768 devices in a mesh: seq: 48 (over y_lo, z, core), fsdp: 16 (over y_hi, x).
Axes of the slice: x: 4, y: 8 (y_hi: 4, y_lo: 2; y = y_hi * 2 + y_lo), z: 12, core: 2. Of those that a mesh axis runs over, the one named last changes fastest.
Arguments:
- queries: bfloat16 [16, 6144, 1024], P('fsdp', 'seq'), may hold values from -6 to 6
- keys: bfloat16 [16, 6144, 1024], P('fsdp', 'seq'), may hold values from -6 to 6
- values: bfloat16 [16, 6144, 1024], P('fsdp', 'seq'), may hold values from -6 to 6
- d_out: bfloat16 [16, 6144, 2048], P('fsdp', 'seq'), may hold values from -6 to 6
- w_out: bfloat16 [1024, 2048], P('fsdp'), may hold values from -0.1875 to 0.1875
- pattern: int32 [48, 4], replicated, may hold values from 0 to 47, as said below
- valid: int32 [16, 48], P('fsdp'), may hold values from 2 to 128, as said below
Outputs:
- d_queries: bfloat16 [16, 6144, 1024], P('fsdp', 'seq')
- d_keys: bfloat16 [16, 6144, 1024], P('fsdp', 'seq')
- d_values: bfloat16 [16, 6144, 1024], P('fsdp', 'seq')
The draws below stay inside these ranges and needn't reach their ends.
Inputs may be any that keep to these rules, and one draw needn't show every extreme that they name: Row b of the pattern, for a query block of shard p, lists the first block of shard p, block b itself, one block of shard p - 1 and one block of shard p + 1; at the first and last shard the missing neighbour's entry repeats the first block of shard p. A block listed twice is attended once. The valid patches of a shard are its first ones; every sample has a shard whose 128 patches are all valid.
All inputs are finite; a program needn't handle non-finite values.
Results may differ from the reference program's by a relative error of at most 0.018.
Values may be sent and summed in bfloat16 or wider, within the bound.
A program may use at most 32 MiB of HBM per device.

```python
import jax
import jax.numpy as jnp
from jax import lax

D = 2048
HEADS = 8
HD = 128
BLOCK = 128
BLK_DEV = 1
TOK_DEV = 128
SEQ = 6144
QBLOCKS = 48
SAMPLES = 16
N_SEQ = 48


def paired_rows(key):
    key_q, key_k = jax.random.split(jax.random.fold_in(key, 7), 2)
    shape = (SAMPLES, SEQ, HEADS * HD)
    query_draw = jnp.clip(jax.random.normal(key_q, shape, jnp.float32), -6.0, 6.0)
    key_draw = jnp.clip(jax.random.normal(key_k, shape, jnp.float32), -6.0, 6.0)
    return (query_draw, key_draw)


def draw_queries(key, part):
    return paired_rows(key)[0].astype(jnp.bfloat16)


def draw_keys(key, part):
    return paired_rows(key)[1].astype(jnp.bfloat16)


def draw_pattern(key, part):
    key_l, key_r = jax.random.split(jax.random.fold_in(key, 13))
    rows = jnp.arange(QBLOCKS, dtype=jnp.int32)
    shard = rows // BLK_DEV
    first = shard * BLK_DEV
    left_pick = jax.random.randint(key_l, (QBLOCKS,), 0, BLK_DEV)
    right_pick = jax.random.randint(key_r, (QBLOCKS,), 0, BLK_DEV)
    left = jnp.where(shard > 0, (shard - 1) * BLK_DEV + left_pick, first)
    right = jnp.where(shard < N_SEQ - 1, (shard + 1) * BLK_DEV + right_pick, first)
    return jnp.stack([first, rows, left, right], axis=1).astype(jnp.int32)


def draw_valid(key, part):
    key_a, key_b = jax.random.split(jax.random.fold_in(key, 11))
    counts = jax.random.randint(key_a, (SAMPLES, N_SEQ), 2, TOK_DEV + 1)
    full = jax.random.randint(key_b, (SAMPLES, 1), 0, N_SEQ)
    return jnp.where(jnp.arange(N_SEQ)[None, :] == full, TOK_DEV, counts).astype(jnp.int32)


def block_scale(rng, dims, cuts, low, top_value):
    gain = 1.0
    for dim, parts in cuts:
        heights = jax.random.uniform(jax.random.fold_in(jax.random.fold_in(rng, 6), dim), (parts,), jnp.float32, low / len(cuts), top_value / len(cuts))
        gain = gain * jnp.repeat(jnp.exp(heights), dims[dim] // parts).reshape((-1,) + (1,) * (len(dims) - 1 - dim))
    return gain


def gaussian(key, shape, scale, most, pieces=(), kind=jnp.bfloat16):
    entries = scale * jax.random.normal(key, shape, jnp.float32)
    if pieces:
        entries = entries * block_scale(key, shape, pieces, -0.22, 0.18)
    return jnp.clip(entries, -most, most).astype(kind)


def setup_inputs(seed: int = 0) -> dict:
    arg_keys = jax.random.split(jax.random.key(seed), 8)
    queries = draw_queries(jax.random.fold_in(arg_keys[7], 71), 0)
    keys = draw_keys(jax.random.fold_in(arg_keys[7], 71), 0)
    values = gaussian(arg_keys[2], (SAMPLES, SEQ, HEADS * HD), 1.0, 6.0, ((0, 16), (1, 48)))
    d_out = gaussian(arg_keys[3], (SAMPLES, SEQ, D), 1.0, 6.0, ((0, 16), (1, 48)))
    w_out = gaussian(arg_keys[4], (HEADS * HD, D), (HEADS * HD) ** -0.5, 0.1875, ((0, 16),))
    pattern = draw_pattern(jax.random.fold_in(arg_keys[7], 71), 0)
    valid = draw_valid(jax.random.fold_in(arg_keys[7], 71), 0)
    return dict(queries=queries, keys=keys, values=values, d_out=d_out, w_out=w_out, pattern=pattern, valid=valid)


def head_split(rows):
    return rows.reshape(rows.shape[0], HEADS, HD)


def allowed_mask(pattern, valid_row, query_shard, key_shard, query_span, key_span, pad_value):
    per_shard = BLK_DEV * BLOCK
    padded = jnp.pad(pattern, ((BLK_DEV, BLK_DEV), (0, 0)), constant_values=pad_value)
    listed_rows = lax.dynamic_slice_in_dim(padded, ((query_shard + 1) * BLK_DEV).astype(jnp.int32), query_span * BLK_DEV, 0)
    key_blocks = key_shard * BLK_DEV + jnp.arange(key_span * BLK_DEV, dtype=jnp.int32)
    listed = jnp.any(listed_rows[:, :, None] == key_blocks[None, None, :], axis=1)
    key_pos = jnp.arange(key_span * per_shard, dtype=jnp.int32)
    owner = key_shard + key_pos // per_shard
    shards = jnp.arange(valid_row.shape[0], dtype=jnp.int32)
    owner_count = jnp.sum(jnp.where(owner[:, None] == shards[None, :], valid_row[None, :], 0), axis=1)
    key_ok = (key_pos % per_shard) < owner_count
    rows_q = query_span * BLK_DEV
    rows_k = key_span * BLK_DEV
    spread = jnp.broadcast_to(listed[:, None, :, None], (rows_q, BLOCK, rows_k, BLOCK))
    return spread.reshape(rows_q * BLOCK, rows_k * BLOCK) & key_ok[None, :]


def block_grads(q_rows, k_rows, v_rows, d_rows, mask):
    scale = HD ** -0.5
    high = lax.Precision.HIGHEST
    q_heads = head_split(q_rows).astype(jnp.float32)
    k_heads = head_split(k_rows).astype(jnp.float32)
    v_heads = head_split(v_rows).astype(jnp.float32)
    d_heads = head_split(d_rows).astype(jnp.float32)
    score = jnp.einsum("qhd,khd->hqk", q_heads, k_heads, precision=high) * scale
    score = jnp.where(mask[None], score, -jnp.inf)
    top = jnp.max(score, axis=2, keepdims=True)
    lse = top + jnp.log(jnp.sum(jnp.exp(score - top), axis=2, keepdims=True))
    prob = jnp.exp(score - lse)
    prob_b = prob.astype(jnp.bfloat16).astype(jnp.float32)
    out = jnp.einsum("hqk,khd->hqd", prob_b, v_heads, precision=high)
    delta = jnp.sum(jnp.transpose(d_heads, (1, 0, 2)) * out, axis=2, keepdims=True)
    d_prob = jnp.einsum("qhd,khd->hqk", d_heads, v_heads, precision=high)
    d_score = (prob * (d_prob - delta)).astype(jnp.bfloat16).astype(jnp.float32)
    d_query = jnp.einsum("hqk,khd->qhd", d_score, k_heads, precision=high) * scale
    key_grad = jnp.einsum("hqk,qhd->khd", d_score, q_heads, precision=high) * scale
    value_grad = jnp.einsum("hqk,qhd->khd", prob_b, d_heads, precision=high)
    width = HEADS * HD
    return (d_query.reshape(-1, width).astype(jnp.bfloat16), key_grad.reshape(-1, width), value_grad.reshape(-1, width))


def reference(queries, keys, values, d_out, w_out, pattern, valid):
    pad_value = -(QBLOCKS + BLK_DEV + 1)
    edge = ((TOK_DEV, TOK_DEV), (0, 0))
    width = HEADS * HD

    def one_sample(items):
        q_all, k_all, v_all, dy_all, valid_row = items
        d_attn = jnp.dot(dy_all, w_out.T, preferred_element_type=jnp.float32).astype(jnp.bfloat16)
        k_pad = jnp.pad(k_all, edge)
        v_pad = jnp.pad(v_all, edge)

        def step(carry, shard):
            key_acc, value_acc = carry
            start = (shard * TOK_DEV).astype(jnp.int32)
            q_rows = lax.dynamic_slice_in_dim(q_all, start, TOK_DEV, 0)
            d_rows = lax.dynamic_slice_in_dim(d_attn, start, TOK_DEV, 0)
            k_band = lax.dynamic_slice_in_dim(k_pad, start, 3 * TOK_DEV, 0)
            v_band = lax.dynamic_slice_in_dim(v_pad, start, 3 * TOK_DEV, 0)
            mask = allowed_mask(pattern, valid_row, shard, shard - 1, 1, 3, pad_value)
            d_query, key_band, value_band = block_grads(q_rows, k_band, v_band, d_rows, mask)
            key_acc = lax.dynamic_update_slice_in_dim(key_acc, lax.dynamic_slice_in_dim(key_acc, start, 3 * TOK_DEV, 0) + key_band, start, 0)
            value_acc = lax.dynamic_update_slice_in_dim(value_acc, lax.dynamic_slice_in_dim(value_acc, start, 3 * TOK_DEV, 0) + value_band, start, 0)
            return (key_acc, value_acc), d_query

        zeros = jnp.zeros((SEQ + 2 * TOK_DEV, width), jnp.float32)
        (key_acc, value_acc), d_query = lax.scan(step, (zeros, zeros), jnp.arange(N_SEQ, dtype=jnp.int32))
        return (d_query.reshape(SEQ, width), key_acc[TOK_DEV:TOK_DEV + SEQ].astype(jnp.bfloat16), value_acc[TOK_DEV:TOK_DEV + SEQ].astype(jnp.bfloat16))

    d_queries, d_keys, d_values = lax.map(one_sample, (queries, keys, values, d_out, valid))
    return (d_queries, d_keys, d_values)
```

```python
import functools

import jax
import jax.numpy as jnp
from jax import lax
from jax.experimental import pallas as pl
from jax.experimental.pallas import tpu as pltpu
from jax.sharding import PartitionSpec as P

HEADS = 8
HD = 128
TOK = 128
N_SEQ = 48
HALF_SEQ = 24
D = 2048
SCALE = HD ** (-0.5)
MESH = pl.DeviceIdType.MESH
ORDER = (0, 1, 3, 2)
BF = jnp.bfloat16
F32 = jnp.float32


def nt(a, b):
    return lax.dot_general(a, b, (((1,), (1,)), ((), ())), preferred_element_type=F32)


def tn(a, b):
    return lax.dot_general(a, b, (((0,), (0,)), ((), ())), preferred_element_type=F32)


def nn(a, b):
    return lax.dot_general(a, b, (((1,), (0,)), ((), ())), preferred_element_type=F32)


def kernel(
    pat_ref, val_ref, q_hbm, k_hbm, v_hbm, do_hbm, w_ref,
    dq_ref, dk_ref, dv_ref,
    q_ref, k_ref, v_ref, do_ref, wf, kh, vh, qh, dh, sth, d_own, st_own, prob, dk_acc, dv_acc,
    wr, sx, sy, ssib, hs_s, hs_r, ds_s, ds_r, ts_s, ts_r, lsem, isem,
):
    p = lax.axis_index("seq")
    f = lax.axis_index("fsdp")
    core = p % 2
    low = p // HALF_SEQ
    k_y = f // 4
    x = f % 4
    sgn = 2 * low - 1
    sib = (p + 1 - 2 * core, f)
    other_y = p + HALF_SEQ * (1 - 2 * low)
    xr = (p, k_y * 4 + (x + 1) % 4)
    xl = (p, k_y * 4 + (x + 3) % 4)
    inter = (other_y, ((k_y + sgn + 4) % 4) * 4 + x)
    intra = (other_y, f)
    opp = (other_y, ((k_y + 2) % 4) * 4 + x)
    has_l = p > 0
    has_r = p < N_SEQ - 1
    left = (p - 1, f)
    right = (p + 1, f)

    loads = [
        pltpu.make_async_copy(a, b, isem.at[i])
        for i, (a, b) in enumerate(
            ((k_hbm, k_ref), (q_hbm, q_ref), (v_hbm, v_ref), (do_hbm, do_ref))
        )
    ]
    own_w = pltpu.make_async_copy(w_ref, wf.at[f], lsem)
    for copy in loads:
        copy.start()
    own_w.start()

    barrier = pltpu.get_barrier_semaphore()
    for dev in (sib, xr, xl, inter, intra, opp):
        pl.semaphore_signal(barrier, inc=1, device_id=dev, device_id_type=MESH)

    @pl.when((core == 0) & has_l)
    def _():
        pl.semaphore_signal(barrier, inc=1, device_id=left, device_id_type=MESH)

    @pl.when((core == 1) & has_r)
    def _():
        pl.semaphore_signal(barrier, inc=1, device_id=right, device_id_type=MESH)

    pl.semaphore_wait(barrier, 5 + (p + N_SEQ - 1) // N_SEQ + (2 * N_SEQ - 2 - p) // N_SEQ)

    def rcopy(src, dst, ssem, rsem, dev):
        return pltpu.make_async_remote_copy(
            src_ref=src, dst_ref=dst, send_sem=ssem, recv_sem=rsem,
            device_id=dev, device_id_type=MESH,
        )

    pending = []

    def put_own(ch, ssem, dev):
        c = rcopy(w_ref.at[ch], wf.at[f, ch], ssem, wr.at[f, ch], dev)
        c.start()
        pending.append(c)

    def put(sh, ch, ssem, dev):
        c = rcopy(wf.at[sh, ch], wf.at[sh, ch], ssem, wr.at[sh, ch], dev)
        c.start()
        pending.append(c)

    def wait_w(sh, ch):
        rcopy(wf.at[sh, ch], wf.at[sh, ch], lsem, wr.at[sh, ch], sib).wait_recv()

    def shard(s, dx):
        return ((k_y + sgn * ORDER[s] + 4) % 4) * 4 + (x + dx) % 4

    mine = (2 * core, 2 * core + 1)
    theirs = (2 - 2 * core, 3 - 2 * core)

    for i in range(2):
        put_own(mine[i], sy.at[i], inter)
        put_own(mine[i], sx.at[0, 0, i], xr)
        put_own(mine[i], sx.at[1, 0, i], xl)
    for i in range(2):
        put_own(mine[i], sy.at[2 + i], opp)

    def halo(i, src, dst, side, dev):
        return rcopy(src.at[0], dst.at[1 - side], hs_s.at[side, i], hs_r.at[1 - side, i], dev)

    halo_parts = ((0, k_hbm, kh), (1, q_hbm, qh), (2, v_hbm, vh))

    @pl.when(has_l)
    def _():
        for i, src, dst in halo_parts:
            halo(i, src, dst, 0, left).start()

    @pl.when(has_r)
    def _():
        for i, src, dst in halo_parts:
            halo(i, src, dst, 1, right).start()

    def clear(side):
        for buf in (kh, vh, qh):
            buf[side] = jnp.zeros((TOK, HEADS * HD), BF)
        dh[side] = jnp.zeros((HEADS, TOK, HD), BF)
        sth[side] = jnp.zeros((HEADS, 8, 128), F32)

    @pl.when(p == 0)
    def _():
        clear(0)

    @pl.when(p == N_SEQ - 1)
    def _():
        clear(1)

    def limit(qb, kb, ok):
        row = (qb + N_SEQ) % N_SEQ
        hit = pat_ref[0, row] == kb
        for i in range(1, 4):
            hit = hit | (pat_ref[i, row] == kb)
        return jnp.where(hit & ok, val_ref[0, (kb + N_SEQ) % N_SEQ], 0)

    lim_own = (limit(p, p - 1, has_l), limit(p, p, p >= 0), limit(p, p + 1, has_r))
    lim_far = (limit(p - 1, p, has_l), limit(p + 1, p, has_r))

    def masked(score, lim):
        rows = lax.broadcasted_iota(jnp.int32, (TOK, TOK), 0)
        return jnp.where(rows < lim, score * SCALE, -jnp.inf)

    def head_of(t):
        s = t // 2
        turn = s + (s // 2) * (1 - 2 * (s % 2))
        return ((k_y + sgn * turn + 4) % 4) * 2 + (x // 2 + t) % 2

    def lanes(h):
        return pl.ds(pl.multiple_of(h * HD, HD), HD)

    def early(t, carry):
        h = head_of(t)
        c = lanes(h)
        q = q_ref[0, :, c]
        s0 = masked(nt(kh[0, :, c], q), lim_own[0])
        s1 = masked(nt(k_ref[0, :, c], q), lim_own[1])
        s2 = masked(nt(kh[1, :, c], q), lim_own[2])
        top = jnp.max(jnp.maximum(jnp.maximum(s0, s1), s2), axis=0, keepdims=True)
        e0, e1, e2 = jnp.exp(s0 - top), jnp.exp(s1 - top), jnp.exp(s2 - top)
        total = jnp.sum(e0 + e1 + e2, axis=0, keepdims=True)
        inv = 1.0 / total
        prob[h, 0] = e0 * inv
        prob[h, 1] = e1 * inv
        prob[h, 2] = e2 * inv
        st_own[h, 0:1, :] = top + jnp.log(total)
        return carry

    def sends(h, fn):
        @pl.when(has_l)
        def _():
            fn(rcopy(d_own.at[h], dh.at[1, h], ds_s.at[0, h], ds_r.at[1, h], left))
            fn(rcopy(st_own.at[h], sth.at[1, h], ts_s.at[0, h], ts_r.at[1, h], left))

        @pl.when(has_r)
        def _():
            fn(rcopy(d_own.at[h], dh.at[0, h], ds_s.at[1, h], ds_r.at[0, h], right))
            fn(rcopy(st_own.at[h], sth.at[0, h], ts_s.at[1, h], ts_r.at[0, h], right))

    def own_head(t, carry):
        h = head_of(t)
        c = lanes(h)
        w_h = wf[pl.ds(2 * h, 2)].reshape(HD, D)
        d = nt(do_ref[0], w_h).astype(BF)
        d_own[h] = d
        dp = (nt(vh[0, :, c], d), nt(v_ref[0, :, c], d), nt(vh[1, :, c], d))
        pr = (prob[h, 0], prob[h, 1], prob[h, 2])
        prb = tuple(a.astype(BF) for a in pr)
        delta = jnp.sum(
            prb[0].astype(F32) * dp[0] + prb[1].astype(F32) * dp[1] + prb[2].astype(F32) * dp[2],
            axis=0, keepdims=True,
        )
        st_own[h, 1:2, :] = delta
        sends(h, lambda copy: copy.start())
        ds = tuple((a * (b - delta)).astype(BF) for a, b in zip(pr, dp))
        k_own = k_ref[0, :, c]
        dq = tn(ds[0], kh[0, :, c]) + tn(ds[1], k_own) + tn(ds[2], kh[1, :, c])
        dq_ref[0, :, c] = (dq * SCALE).astype(BF)
        dk_acc[h] = nn(ds[1], q_ref[0, :, c])
        dv_acc[h] = nn(prb[1], d)
        return carry

    def far_head(t, carry):
        h = head_of(t)
        c = lanes(h)

        @pl.when(has_l)
        def _():
            rcopy(d_own.at[h], dh.at[0, h], ds_s.at[1, h], ds_r.at[0, h], sib).wait_recv()
            rcopy(st_own.at[h], sth.at[0, h], ts_s.at[1, h], ts_r.at[0, h], sib).wait_recv()

        @pl.when(has_r)
        def _():
            rcopy(d_own.at[h], dh.at[1, h], ds_s.at[0, h], ds_r.at[1, h], sib).wait_recv()
            rcopy(st_own.at[h], sth.at[1, h], ts_s.at[0, h], ts_r.at[1, h], sib).wait_recv()

        k_own = k_ref[0, :, c]
        v_own = v_ref[0, :, c]
        dk = dk_acc[h]
        dv = dv_acc[h]
        for side in range(2):
            q = qh[side, :, c]
            d = dh[side, h]
            pr = jnp.exp(masked(nt(k_own, q), lim_far[side]) - sth[side, h, 0:1, :])
            ds = (pr * (nt(v_own, d) - sth[side, h, 1:2, :])).astype(BF)
            dk = dk + nn(ds, q)
            dv = dv + nn(pr.astype(BF), d)
        dk_ref[0, :, c] = (dk * SCALE).astype(BF)
        dv_ref[0, :, c] = dv.astype(BF)
        return carry

    def wait_halo():
        @pl.when(has_l)
        def _():
            for i, src, dst in halo_parts:
                rcopy(src.at[0], dst.at[0], hs_s.at[1, i], hs_r.at[0, i], sib).wait_recv()

        @pl.when(has_r)
        def _():
            for i, src, dst in halo_parts:
                rcopy(src.at[0], dst.at[1], hs_s.at[0, i], hs_r.at[1, i], sib).wait_recv()

    def y_round(s):
        for i in range(2):
            sh, ch = shard(s, 0), mine[i]
            wait_w(sh, ch)
            if s == 1:
                put(sh, ch, sy.at[4 + i], intra)
            put(sh, ch, sx.at[0, s, i], xr)
            put(sh, ch, sx.at[1, s, i], xl)
            put(sh, ch, ssib.at[s, i], sib)

    def x_round(s):
        for i in range(2):
            for side, dx in ((0, 3), (1, 1)):
                sh, ch = shard(s, dx), mine[i]
                wait_w(sh, ch)
                if i == side:
                    put(sh, ch, sx.at[side, s, 2], xr if side == 0 else xl)
                put(sh, ch, ssib.at[s, 2 + 2 * side + i], sib)

    def far_round(s):
        for i in range(2):
            sh, ch = shard(s, 2), mine[i]
            wait_w(sh, ch)
            put(sh, ch, ssib.at[s, 6 + i], sib)

    def sib_round(s, which):
        for dx in which:
            if s == 0 and dx == 0:
                continue
            for i in range(2):
                wait_w(shard(s, dx), theirs[i])

    y_round(1)
    x_round(0)
    y_round(2)
    for copy in loads:
        copy.wait()
    wait_halo()
    lax.fori_loop(0, 2, early, 0)
    x_round(1)
    y_round(3)
    far_round(0)
    own_w.wait()
    sib_round(0, (0, 1, 2, 3))
    lax.fori_loop(0, 2, own_head, 0)
    x_round(2)
    far_round(1)
    lax.fori_loop(2, 6, early, 0)
    sib_round(1, (0, 1, 2, 3))
    lax.fori_loop(2, 4, own_head, 0)
    lax.fori_loop(0, 2, far_head, 0)
    x_round(3)
    far_round(2)
    lax.fori_loop(6, 8, early, 0)
    sib_round(2, (0, 1, 2, 3))
    lax.fori_loop(4, 6, own_head, 0)
    far_round(3)
    lax.fori_loop(2, 6, far_head, 0)
    sib_round(3, (0, 1, 2, 3))
    lax.fori_loop(6, 8, own_head, 0)
    lax.fori_loop(6, 8, far_head, 0)

    for c in pending:
        c.wait_send()

    @pl.when(has_l)
    def _():
        for i, src, dst in halo_parts:
            halo(i, src, dst, 0, left).wait_send()

    @pl.when(has_r)
    def _():
        for i, src, dst in halo_parts:
            halo(i, src, dst, 1, right).wait_send()

    def drain(h, carry):
        sends(h, lambda copy: copy.wait_send())
        return carry

    lax.fori_loop(0, HEADS, drain, 0)


def body(queries, keys, values, d_out, w_out, pattern, valid):
    tok, width = queries.shape[1], queries.shape[2]
    vm = pl.BlockSpec(memory_space=pltpu.VMEM)
    sm = pl.BlockSpec(memory_space=pltpu.SMEM)
    hbm = pl.BlockSpec(memory_space=pltpu.HBM)
    out = jax.ShapeDtypeStruct((1, tok, width), BF)
    dma = pltpu.SemaphoreType.DMA
    return pl.pallas_call(
        kernel,
        out_shape=(out, out, out),
        in_specs=[sm, sm, hbm, hbm, hbm, hbm, hbm],
        out_specs=(vm, vm, vm),
        scratch_shapes=[
            pltpu.VMEM((1, tok, width), BF),
            pltpu.VMEM((1, tok, width), BF),
            pltpu.VMEM((1, tok, width), BF),
            pltpu.VMEM((1, tok, D), BF),
            pltpu.VMEM((16, 4, 16, D), BF),
            pltpu.VMEM((2, tok, width), BF),
            pltpu.VMEM((2, tok, width), BF),
            pltpu.VMEM((2, tok, width), BF),
            pltpu.VMEM((2, HEADS, tok, HD), BF),
            pltpu.VMEM((2, HEADS, 8, 128), F32),
            pltpu.VMEM((HEADS, tok, HD), BF),
            pltpu.VMEM((HEADS, 8, 128), F32),
            pltpu.VMEM((HEADS, 3, tok, tok), F32),
            pltpu.VMEM((HEADS, tok, HD), F32),
            pltpu.VMEM((HEADS, tok, HD), F32),
            dma((16, 4)),
            dma((2, 4, 3)),
            dma((6,)),
            dma((4, 8)),
            dma((2, 3)),
            dma((2, 3)),
            dma((2, HEADS)),
            dma((2, HEADS)),
            dma((2, HEADS)),
            dma((2, HEADS)),
            dma,
            dma((4,)),
        ],
        compiler_params=pltpu.CompilerParams(
            collective_id=0, has_side_effects=True
        ),
        name="attention_backward",
    )(pattern.T, valid, queries, keys, values, d_out, w_out.reshape(4, 16, D))


def solution(mesh):
    spec = P("fsdp", "seq", None)
    in_specs = (spec, spec, spec, spec, P("fsdp", None), P(), P("fsdp", None))
    return jax.shard_map(
        body, mesh=mesh, in_specs=in_specs, out_specs=(spec, spec, spec), check_vma=False
    )
```

```python
import functools

import jax
import jax.numpy as jnp
from jax import lax
from jax.experimental import pallas as pl
from jax.experimental.pallas import tpu as pltpu
from jax.sharding import PartitionSpec as P

HEADS = 8
HD = 128
TOK = 128
N_SEQ = 48
HALF_SEQ = 24
D = 2048
SCALE = HD ** (-0.5)
MESH = pl.DeviceIdType.MESH
ORDER = (0, 1, 3, 2)
BF = jnp.bfloat16
F32 = jnp.float32


def nt(a, b):
    return lax.dot_general(a, b, (((1,), (1,)), ((), ())), preferred_element_type=F32)


def tn(a, b):
    return lax.dot_general(a, b, (((0,), (0,)), ((), ())), preferred_element_type=F32)


def nn(a, b):
    return lax.dot_general(a, b, (((1,), (0,)), ((), ())), preferred_element_type=F32)


def kernel(
    pat_ref, val_ref, q_hbm, k_hbm, v_hbm, do_hbm, w_ref,
    dq_ref, dk_ref, dv_ref,
    qb, kb, vb, do_ref, wf, dh, sth, d_own, st_own, prob, dk_acc, dv_acc, rel,
    wr, sx, sy, ssib, hs_s, hs_r, ds_s, ds_r, ts_s, ts_r, lsem, isem, ready, rel_r,
):
    p = lax.axis_index("seq")
    f = lax.axis_index("fsdp")
    core = p % 2
    low = p // HALF_SEQ
    k_y = f // 4
    x = f % 4
    sgn = 2 * low - 1
    sib = (p + 1 - 2 * core, f)
    zdev = (p - 1 + 2 * core, f)
    other_y = p + HALF_SEQ * (1 - 2 * low)
    xr = (p, k_y * 4 + (x + 1) % 4)
    xl = (p, k_y * 4 + (x + 3) % 4)
    inter = (other_y, ((k_y + sgn + 4) % 4) * 4 + x)
    intra = (other_y, f)
    opp = (other_y, ((k_y + 2) % 4) * 4 + x)
    has_l = p > 0
    has_r = p < N_SEQ - 1
    has_z = has_l & has_r
    wrap_lo = p == HALF_SEQ - 1
    wrap_hi = p == HALF_SEQ
    relays = p == 0
    wrap_dev = (HALF_SEQ - 1, f)
    greets_last = has_z & (((core == 0) & (p != HALF_SEQ)) | wrap_lo)
    greets_first = has_z & (((core == 1) & (p != HALF_SEQ - 1)) | wrap_hi)

    loads = [
        pltpu.make_async_copy(a, b, isem.at[i])
        for i, (a, b) in enumerate(
            (
                (k_hbm.at[0], kb.at[1]),
                (q_hbm.at[0], qb.at[1]),
                (v_hbm.at[0], vb.at[1]),
                (do_hbm.at[0], do_ref),
            )
        )
    ]
    own_w = pltpu.make_async_copy(w_ref, wf.at[f], lsem)
    for copy in loads:
        copy.start()
    own_w.start()

    barrier = pltpu.get_barrier_semaphore()
    for dev in (sib, xr, xl, inter, intra, opp):
        pl.semaphore_signal(barrier, inc=1, device_id=dev, device_id_type=MESH)

    @pl.when(greets_first)
    def _():
        pl.semaphore_signal(barrier, inc=1, device_id=zdev, device_id_type=MESH)

    @pl.when(relays)
    def _():
        pl.semaphore_signal(barrier, inc=1, device_id=wrap_dev, device_id_type=MESH)

    @pl.when(greets_last & ~wrap_lo)
    def _():
        pl.semaphore_wait(barrier, 7)
        pl.semaphore_signal(ready, inc=1, device_id=zdev, device_id_type=MESH)

    @pl.when(wrap_lo)
    def _():
        pl.semaphore_wait(barrier, 8)
        for dev in (zdev, (0, f)):
            pl.semaphore_signal(ready, inc=1, device_id=dev, device_id_type=MESH)

    @pl.when(~greets_last)
    def _():
        pl.semaphore_wait(barrier, 6)

    def rcopy(src, dst, ssem, rsem, dev):
        return pltpu.make_async_remote_copy(
            src_ref=src, dst_ref=dst, send_sem=ssem, recv_sem=rsem,
            device_id=dev, device_id_type=MESH,
        )

    pending = []

    def put_own(ch, ssem, dev):
        c = rcopy(w_ref.at[ch], wf.at[f, ch], ssem, wr.at[f, ch], dev)
        c.start()
        pending.append(c)

    def put(sh, ch, ssem, dev):
        c = rcopy(wf.at[sh, ch], wf.at[sh, ch], ssem, wr.at[sh, ch], dev)
        c.start()
        pending.append(c)

    def wait_w(sh, ch):
        rcopy(wf.at[sh, ch], wf.at[sh, ch], lsem, wr.at[sh, ch], sib).wait_recv()

    def shard(s, dx):
        return ((k_y + sgn * ORDER[s] + 4) % 4) * 4 + (x + dx) % 4

    mine = (2 * core, 2 * core + 1)
    theirs = (2 - 2 * core, 3 - 2 * core)

    for i in range(2):
        put_own(mine[i], sy.at[i], inter)
        put_own(mine[i], sx.at[0, 0, i], xr)
        put_own(mine[i], sx.at[1, 0, i], xl)
    for i in range(2):
        put_own(mine[i], sy.at[2 + i], opp)

    halo_parts = ((0, k_hbm, kb), (1, v_hbm, vb), (2, q_hbm, qb))

    def halo(i, src, dst, side, dev):
        return rcopy(
            src.at[0], dst.at[2 - 2 * side], hs_s.at[side, i], hs_r.at[1 - side, i], dev
        )

    def halo_to(side, dev):
        for i, src, dst in halo_parts:
            halo(i, src, dst, side, dev).start()

    halo_to(1 - core, sib)

    @pl.when(greets_last)
    def _():
        halo_to(core, zdev)

    @pl.when(greets_first & (p != HALF_SEQ))
    def _():
        pl.semaphore_wait(ready, 1)
        halo_to(core, zdev)

    def to_relay(i):
        return rcopy(halo_parts[i][1].at[0], rel.at[i], hs_s.at[0, i], rel_r.at[i], intra)

    def relay(i):
        dst = halo_parts[i][2].at[2]
        return rcopy(rel.at[i], dst, hs_s.at[0, i], hs_r.at[1, i], wrap_dev)

    def pass_on(i):
        @pl.when(relays)
        def _():
            if i == 0:
                pl.semaphore_wait(ready, 1)
            to_relay(i).wait_recv()
            relay(i).start()

    def wait_halo(which):
        for i in which:
            halo(*halo_parts[i], core, sib).wait_recv()

        @pl.when(has_z)
        def _():
            for i in which:
                halo(*halo_parts[i], 1 - core, sib).wait_recv()

    @pl.when(~has_z)
    def _():
        for buf in (kb, vb, qb):
            buf[2 * core] = jnp.zeros((TOK, HEADS * HD), BF)
        dh[core] = jnp.zeros((HEADS, TOK, HD), BF)
        sth[core] = jnp.zeros((HEADS, 8, 128), F32)

    def limit(qblock, kblock, ok):
        row = (qblock + N_SEQ) % N_SEQ
        hit = pat_ref[0, row] == kblock
        for i in range(1, 4):
            hit = hit | (pat_ref[i, row] == kblock)
        return jnp.where(hit & ok, val_ref[0, (kblock + N_SEQ) % N_SEQ], 0)

    lim_own = (limit(p, p - 1, has_l), limit(p, p, p >= 0), limit(p, p + 1, has_r))
    lim_far = (limit(p - 1, p, has_l), limit(p + 1, p, has_r))

    def masked(score, lim):
        rows = lax.broadcasted_iota(jnp.int32, (TOK, TOK), 0)
        return jnp.where(rows < lim, score * SCALE, -jnp.inf)

    def head_of(t):
        s = t // 2
        turn = s + (s // 2) * (1 - 2 * (s % 2))
        return ((k_y + sgn * turn + 4) % 4) * 2 + (x // 2 + t) % 2

    def lanes(h):
        return pl.ds(pl.multiple_of(h * HD, HD), HD)

    def thirds(a):
        return a[:TOK], a[TOK : 2 * TOK], a[2 * TOK :]

    def early(t, carry):
        h = head_of(t)
        c = lanes(h)
        score = nt(kb[:, :, c].reshape(3 * TOK, HD), qb[1, :, c])
        s0, s1, s2 = (masked(a, lim) for a, lim in zip(thirds(score), lim_own))
        top = jnp.max(jnp.maximum(jnp.maximum(s0, s1), s2), axis=0, keepdims=True)
        e0, e1, e2 = jnp.exp(s0 - top), jnp.exp(s1 - top), jnp.exp(s2 - top)
        total = jnp.sum(e0 + e1 + e2, axis=0, keepdims=True)
        inv = 1.0 / total
        prob[h, 0:TOK] = e0 * inv
        prob[h, TOK : 2 * TOK] = e1 * inv
        prob[h, 2 * TOK :] = e2 * inv
        st_own[h, 0:1, :] = top + jnp.log(total)
        return carry

    def send_d(h, side, dev):
        return (
            rcopy(d_own.at[h], dh.at[1 - side, h], ds_s.at[side, h], ds_r.at[1 - side, h], dev),
            rcopy(st_own.at[h], sth.at[1 - side, h], ts_s.at[side, h], ts_r.at[1 - side, h], dev),
        )

    def own_head(t, carry):
        h = head_of(t)
        c = lanes(h)
        w_h = wf[pl.ds(2 * h, 2)].reshape(HD, D)
        d = nt(do_ref[...], w_h).astype(BF)
        d_own[h] = d
        dp = nt(vb[:, :, c].reshape(3 * TOK, HD), d)
        pr = prob[h]
        prb = pr.astype(BF)
        delta = jnp.sum(prb.astype(F32) * dp, axis=0, keepdims=True)
        st_own[h, 1:2, :] = delta

        @pl.when(has_z)
        def _():
            for copy in send_d(h, core, zdev):
                copy.start()

        for copy in send_d(h, 1 - core, sib):
            copy.start()
        ds = (pr * (dp - delta)).astype(BF)
        dq = tn(ds, kb[:, :, c].reshape(3 * TOK, HD))
        dq_ref[0, :, c] = (dq * SCALE).astype(BF)
        dk_acc[h] = nn(ds[TOK : 2 * TOK], qb[1, :, c])
        dv_acc[h] = nn(prb[TOK : 2 * TOK], d)
        return carry

    def far_head(t, carry):
        h = head_of(t)
        c = lanes(h)
        for copy in send_d(h, core, sib):
            copy.wait_recv()

        @pl.when(has_z)
        def _():
            for copy in send_d(h, 1 - core, sib):
                copy.wait_recv()

        q = jnp.concatenate([qb[0, :, c], qb[2, :, c]], axis=0)
        d = dh[:, h].reshape(2 * TOK, HD)
        score = nt(kb[1, :, c], q)
        dp = nt(vb[1, :, c], d)
        pr, ds = [], []
        for side in range(2):
            cols = slice(side * TOK, (side + 1) * TOK)
            a = jnp.exp(masked(score[:, cols], lim_far[side]) - sth[side, h, 0:1, :])
            pr.append(a.astype(BF))
            ds.append((a * (dp[:, cols] - sth[side, h, 1:2, :])).astype(BF))
        dk = dk_acc[h] + nn(jnp.concatenate(ds, axis=1), q)
        dv = dv_acc[h] + nn(jnp.concatenate(pr, axis=1), d)
        dk_ref[0, :, c] = (dk * SCALE).astype(BF)
        dv_ref[0, :, c] = dv.astype(BF)
        return carry

    def y_round(s):
        for i in range(2):
            sh, ch = shard(s, 0), mine[i]
            wait_w(sh, ch)
            if s == 1:
                put(sh, ch, sy.at[4 + i], intra)
            put(sh, ch, sx.at[0, s, i], xr)
            put(sh, ch, sx.at[1, s, i], xl)
            put(sh, ch, ssib.at[s, i], sib)

    def x_round(s):
        for i in range(2):
            for side, dx in ((0, 3), (1, 1)):
                sh, ch = shard(s, dx), mine[i]
                wait_w(sh, ch)
                if i == side:
                    put(sh, ch, sx.at[side, s, 2], xr if side == 0 else xl)
                put(sh, ch, ssib.at[s, 2 + 2 * side + i], sib)

    def far_round(s):
        for i in range(2):
            sh, ch = shard(s, 2), mine[i]
            wait_w(sh, ch)
            put(sh, ch, ssib.at[s, 6 + i], sib)

    def sib_round(s):
        for dx in range(4):
            if s == 0 and dx == 0:
                continue
            for i in range(2):
                wait_w(shard(s, dx), theirs[i])

    past = wrap_hi.astype(jnp.int32)
    past_far = ((p // 2 == HALF_SEQ // 2) | wrap_lo).astype(jnp.int32)

    def run(fn, usual, other, which=past):
        lo = usual[0] * (1 - which) + other[0] * which
        hi = usual[1] * (1 - which) + other[1] * which
        lax.fori_loop(lo, hi, fn, 0)

    def halo_if(cond, i):
        @pl.when(cond)
        def _():
            wait_halo((i,))

    y_round(1)

    @pl.when(wrap_hi)
    def _():
        for i in range(3):
            to_relay(i).start()

    x_round(0)
    y_round(2)
    x_round(1)

    for copy in loads:
        copy.wait()
    halo_if(~wrap_hi, 0)
    run(early, (0, 4), (0, 0))
    y_round(3)
    far_round(0)
    pass_on(0)
    run(early, (4, 8), (0, 0))
    own_w.wait()
    sib_round(0)
    halo_if(~wrap_hi, 1)

    run(own_head, (0, 2), (0, 0))
    x_round(2)
    far_round(1)
    pass_on(1)
    sib_round(1)
    halo_if(wrap_hi, 0)
    run(early, (8, 8), (0, 8))
    run(own_head, (2, 4), (0, 0))
    x_round(3)
    far_round(2)
    pass_on(2)
    halo_if(~wrap_hi, 2)
    halo_if(wrap_hi, 1)

    @pl.when(wrap_hi)
    def _():
        pl.semaphore_wait(ready, 1)

    run(own_head, (4, 4), (0, 4))
    run(far_head, (0, 2), (0, 0), past_far)
    sib_round(2)
    run(own_head, (4, 6), (4, 6))
    far_round(3)
    halo_if(wrap_hi, 2)

    run(far_head, (2, 4), (0, 0), past_far)
    sib_round(3)
    run(own_head, (6, 8), (6, 8))

    run(far_head, (4, 8), (0, 8), past_far)

    for c in pending:
        c.wait_send()
    for part in halo_parts:
        halo(*part, 1 - core, sib).wait_send()

    @pl.when(has_z)
    def _():
        for part in halo_parts:
            halo(*part, core, zdev).wait_send()

    @pl.when(relays)
    def _():
        for i in range(3):
            relay(i).wait_send()

    def drain(h, carry):
        for copy in send_d(h, 1 - core, sib):
            copy.wait_send()

        @pl.when(has_z)
        def _():
            for copy in send_d(h, core, zdev):
                copy.wait_send()

        return carry

    lax.fori_loop(0, HEADS, drain, 0)


def body(queries, keys, values, d_out, w_out, pattern, valid):
    tok, width = queries.shape[1], queries.shape[2]
    vm = pl.BlockSpec(memory_space=pltpu.VMEM)
    sm = pl.BlockSpec(memory_space=pltpu.SMEM)
    hbm = pl.BlockSpec(memory_space=pltpu.HBM)
    out = jax.ShapeDtypeStruct((1, tok, width), BF)
    dma = pltpu.SemaphoreType.DMA
    return pl.pallas_call(
        kernel,
        out_shape=(out, out, out),
        in_specs=[sm, sm, hbm, hbm, hbm, hbm, hbm],
        out_specs=(vm, vm, vm),
        scratch_shapes=[
            pltpu.VMEM((3, tok, width), BF),
            pltpu.VMEM((3, tok, width), BF),
            pltpu.VMEM((3, tok, width), BF),
            pltpu.VMEM((tok, D), BF),
            pltpu.VMEM((16, 4, 16, D), BF),
            pltpu.VMEM((2, HEADS, tok, HD), BF),
            pltpu.VMEM((2, HEADS, 8, 128), F32),
            pltpu.VMEM((HEADS, tok, HD), BF),
            pltpu.VMEM((HEADS, 8, 128), F32),
            pltpu.VMEM((HEADS, 3 * tok, tok), F32),
            pltpu.VMEM((HEADS, tok, HD), F32),
            pltpu.VMEM((HEADS, tok, HD), F32),
            pltpu.VMEM((3, tok, width), BF),
            dma((16, 4)),
            dma((2, 4, 3)),
            dma((6,)),
            dma((4, 8)),
            dma((2, 3)),
            dma((2, 3)),
            dma((2, HEADS)),
            dma((2, HEADS)),
            dma((2, HEADS)),
            dma((2, HEADS)),
            dma,
            dma((4,)),
            pltpu.SemaphoreType.REGULAR,
            dma((3,)),
        ],
        compiler_params=pltpu.CompilerParams(
            collective_id=0, has_side_effects=True
        ),
        name="attention_backward",
    )(pattern.T, valid, queries, keys, values, d_out, w_out.reshape(4, 16, D))


def solution(mesh):
    spec = P("fsdp", "seq", None)
    in_specs = (spec, spec, spec, spec, P("fsdp", None), P(), P("fsdp", None))
    return jax.shard_map(
        body, mesh=mesh, in_specs=in_specs, out_specs=(spec, spec, spec), check_vma=False
    )
```

```python
import functools

import jax
import jax.numpy as jnp
from jax import lax
from jax.experimental import pallas as pl
from jax.experimental.pallas import tpu as pltpu
from jax.sharding import PartitionSpec as P

HEADS = 8
HD = 128
TOK = 128
N_SEQ = 48
HALF_SEQ = 24
D = 2048
SCALE = HD ** (-0.5)
MESH = pl.DeviceIdType.MESH
ORDER = (0, 1, 3, 2)
BF = jnp.bfloat16
F32 = jnp.float32


def nt(a, b):
    return lax.dot_general(a, b, (((1,), (1,)), ((), ())), preferred_element_type=F32)


def tn(a, b):
    return lax.dot_general(a, b, (((0,), (0,)), ((), ())), preferred_element_type=F32)


def nn(a, b):
    return lax.dot_general(a, b, (((1,), (0,)), ((), ())), preferred_element_type=F32)


def kernel(
    pat_ref, val_ref, q_hbm, k_hbm, v_hbm, do_hbm, w_ref,
    dq_ref, dk_ref, dv_ref,
    qb, kb, vb, do_ref, wf, dh, sth, d_own, st_own, prob, dk_acc, dv_acc, rel,
    wr, sx, sy, ssib, hs_s, hs_r, ds_s, ds_r, ts_s, ts_r, lsem, isem, ready, rel_r,
):
    p = lax.axis_index("seq")
    f = lax.axis_index("fsdp")
    core = p % 2
    low = p // HALF_SEQ
    k_y = f // 4
    x = f % 4
    sgn = 2 * low - 1
    sib = (p + 1 - 2 * core, f)
    zdev = (p - 1 + 2 * core, f)
    other_y = p + HALF_SEQ * (1 - 2 * low)
    xr = (p, k_y * 4 + (x + 1) % 4)
    xl = (p, k_y * 4 + (x + 3) % 4)
    inter = (other_y, ((k_y + sgn + 4) % 4) * 4 + x)
    intra = (other_y, f)
    opp = (other_y, ((k_y + 2) % 4) * 4 + x)
    has_l = p > 0
    has_r = p < N_SEQ - 1
    has_z = has_l & has_r
    wrap_lo = p == HALF_SEQ - 1
    wrap_hi = p == HALF_SEQ
    relays = p == 0
    wrap_dev = (HALF_SEQ - 1, f)
    greets_last = has_z & (((core == 0) & (p != HALF_SEQ)) | wrap_lo)
    greets_first = has_z & (((core == 1) & (p != HALF_SEQ - 1)) | wrap_hi)

    loads = [
        pltpu.make_async_copy(a, b, isem.at[i])
        for i, (a, b) in enumerate(
            (
                (k_hbm.at[0], kb.at[1]),
                (q_hbm.at[0], qb.at[1]),
                (v_hbm.at[0], vb.at[1]),
                (do_hbm.at[0], do_ref),
            )
        )
    ]
    own_w = pltpu.make_async_copy(w_ref, wf.at[f], lsem)
    for copy in loads:
        copy.start()
    own_w.start()

    barrier = pltpu.get_barrier_semaphore()
    for dev in (sib, xr, xl, inter, intra, opp):
        pl.semaphore_signal(barrier, inc=1, device_id=dev, device_id_type=MESH)

    @pl.when(greets_first)
    def _():
        pl.semaphore_signal(barrier, inc=1, device_id=zdev, device_id_type=MESH)

    @pl.when(relays)
    def _():
        pl.semaphore_signal(barrier, inc=1, device_id=wrap_dev, device_id_type=MESH)

    @pl.when(greets_last & ~wrap_lo)
    def _():
        pl.semaphore_wait(barrier, 7)
        pl.semaphore_signal(ready, inc=1, device_id=zdev, device_id_type=MESH)

    @pl.when(wrap_lo)
    def _():
        pl.semaphore_wait(barrier, 8)
        for dev in (zdev, (0, f)):
            pl.semaphore_signal(ready, inc=1, device_id=dev, device_id_type=MESH)

    @pl.when(~greets_last)
    def _():
        pl.semaphore_wait(barrier, 6)

    def rcopy(src, dst, ssem, rsem, dev):
        return pltpu.make_async_remote_copy(
            src_ref=src, dst_ref=dst, send_sem=ssem, recv_sem=rsem,
            device_id=dev, device_id_type=MESH,
        )

    pending = []

    def put_own(ch, ssem, dev):
        c = rcopy(w_ref.at[ch], wf.at[f, ch], ssem, wr.at[f, ch], dev)
        c.start()
        pending.append(c)

    def put(sh, ch, ssem, dev):
        c = rcopy(wf.at[sh, ch], wf.at[sh, ch], ssem, wr.at[sh, ch], dev)
        c.start()
        pending.append(c)

    def wait_w(sh, ch):
        rcopy(wf.at[sh, ch], wf.at[sh, ch], lsem, wr.at[sh, ch], sib).wait_recv()

    def shard(s, dx):
        return ((k_y + sgn * ORDER[s] + 4) % 4) * 4 + (x + dx) % 4

    mine = (2 * core, 2 * core + 1)
    theirs = (2 - 2 * core, 3 - 2 * core)

    for i in range(2):
        put_own(mine[i], sy.at[i], inter)
        put_own(mine[i], sx.at[0, 0, i], xr)
        put_own(mine[i], sx.at[1, 0, i], xl)
    for i in range(2):
        put_own(mine[i], sy.at[2 + i], opp)

    halo_parts = ((0, k_hbm, kb), (1, v_hbm, vb), (2, q_hbm, qb))

    def halo(i, src, dst, side, dev):
        return rcopy(
            src.at[0], dst.at[2 - 2 * side], hs_s.at[side, i], hs_r.at[1 - side, i], dev
        )

    def halo_to(side, dev):
        for i, src, dst in halo_parts:
            halo(i, src, dst, side, dev).start()

    halo_to(1 - core, sib)

    @pl.when(greets_last)
    def _():
        halo_to(core, zdev)

    @pl.when(greets_first & (p != HALF_SEQ))
    def _():
        pl.semaphore_wait(ready, 1)
        halo_to(core, zdev)

    def to_relay(i):
        return rcopy(halo_parts[i][1].at[0], rel.at[i], hs_s.at[0, i], rel_r.at[i], intra)

    def relay(i):
        dst = halo_parts[i][2].at[2]
        return rcopy(rel.at[i], dst, hs_s.at[0, i], hs_r.at[1, i], wrap_dev)

    def pass_on(i):
        @pl.when(relays)
        def _():
            if i == 0:
                pl.semaphore_wait(ready, 1)
            to_relay(i).wait_recv()
            relay(i).start()

    def wait_halo(which):
        for i in which:
            halo(*halo_parts[i], core, sib).wait_recv()

        @pl.when(has_z)
        def _():
            for i in which:
                halo(*halo_parts[i], 1 - core, sib).wait_recv()

    @pl.when(~has_z)
    def _():
        for buf in (kb, vb, qb):
            buf[2 * core] = jnp.zeros((TOK, HEADS * HD), BF)
        dh[core] = jnp.zeros((HEADS, TOK, HD), BF)
        sth[core] = jnp.zeros((HEADS, 8, 128), F32)

    def limit(qblock, kblock, ok):
        row = (qblock + N_SEQ) % N_SEQ
        hit = pat_ref[0, row] == kblock
        for i in range(1, 4):
            hit = hit | (pat_ref[i, row] == kblock)
        return jnp.where(hit & ok, val_ref[0, (kblock + N_SEQ) % N_SEQ], 0)

    lim_own = (limit(p, p - 1, has_l), limit(p, p, p >= 0), limit(p, p + 1, has_r))
    lim_far = (limit(p - 1, p, has_l), limit(p + 1, p, has_r))

    def masked(score, lim):
        rows = lax.broadcasted_iota(jnp.int32, (TOK, TOK), 0)
        return jnp.where(rows < lim, score * SCALE, -jnp.inf)

    def head_of(t):
        s = t // 2
        turn = s + (s // 2) * (1 - 2 * (s % 2))
        return ((k_y + sgn * turn + 4) % 4) * 2 + (x // 2 + t) % 2

    def lanes(h):
        return pl.ds(pl.multiple_of(h * HD, HD), HD)

    def thirds(a):
        return a[:TOK], a[TOK : 2 * TOK], a[2 * TOK :]

    def early(t, carry):
        h = head_of(t)
        c = lanes(h)
        score = nt(kb[:, :, c].reshape(3 * TOK, HD), qb[1, :, c])
        s0, s1, s2 = (masked(a, lim) for a, lim in zip(thirds(score), lim_own))
        top = jnp.max(jnp.maximum(jnp.maximum(s0, s1), s2), axis=0, keepdims=True)
        e0, e1, e2 = jnp.exp(s0 - top), jnp.exp(s1 - top), jnp.exp(s2 - top)
        total = jnp.sum(e0 + e1 + e2, axis=0, keepdims=True)
        inv = 1.0 / total
        prob[h, 0:TOK] = e0 * inv
        prob[h, TOK : 2 * TOK] = e1 * inv
        prob[h, 2 * TOK :] = e2 * inv
        st_own[h, 0:1, :] = top + jnp.log(total)
        return carry

    def send_d(h, side, dev):
        return (
            rcopy(d_own.at[h], dh.at[1 - side, h], ds_s.at[side, h], ds_r.at[1 - side, h], dev),
            rcopy(st_own.at[h], sth.at[1 - side, h], ts_s.at[side, h], ts_r.at[1 - side, h], dev),
        )

    def own_head(t, carry):
        h = head_of(t)
        c = lanes(h)
        w_h = wf[pl.ds(2 * h, 2)].reshape(HD, D)
        d = nt(do_ref[...], w_h).astype(BF)
        d_own[h] = d
        dp = nt(vb[:, :, c].reshape(3 * TOK, HD), d)
        pr = prob[h]
        prb = pr.astype(BF)
        delta = jnp.sum(prb.astype(F32) * dp, axis=0, keepdims=True)
        st_own[h, 1:2, :] = delta

        @pl.when(has_z)
        def _():
            for copy in send_d(h, core, zdev):
                copy.start()

        for copy in send_d(h, 1 - core, sib):
            copy.start()
        ds = (pr * (dp - delta)).astype(BF)
        dq = tn(ds, kb[:, :, c].reshape(3 * TOK, HD))
        dq_ref[0, :, c] = (dq * SCALE).astype(BF)
        dk_acc[h] = nn(ds[TOK : 2 * TOK], qb[1, :, c])
        dv_acc[h] = nn(prb[TOK : 2 * TOK], d)
        return carry

    def far_head(t, carry):
        h = head_of(t)
        c = lanes(h)
        for copy in send_d(h, core, sib):
            copy.wait_recv()

        @pl.when(has_z)
        def _():
            for copy in send_d(h, 1 - core, sib):
                copy.wait_recv()

        q = jnp.concatenate([qb[0, :, c], qb[2, :, c]], axis=0)
        d = dh[:, h].reshape(2 * TOK, HD)
        score = nt(kb[1, :, c], q)
        dp = nt(vb[1, :, c], d)
        pr, ds = [], []
        for side in range(2):
            cols = slice(side * TOK, (side + 1) * TOK)
            a = jnp.exp(masked(score[:, cols], lim_far[side]) - sth[side, h, 0:1, :])
            pr.append(a.astype(BF))
            ds.append((a * (dp[:, cols] - sth[side, h, 1:2, :])).astype(BF))
        dk = dk_acc[h] + nn(jnp.concatenate(ds, axis=1), q)
        dv = dv_acc[h] + nn(jnp.concatenate(pr, axis=1), d)
        dk_ref[0, :, c] = (dk * SCALE).astype(BF)
        dv_ref[0, :, c] = dv.astype(BF)
        return carry

    def y_round(s):
        for i in range(2):
            sh, ch = shard(s, 0), mine[i]
            wait_w(sh, ch)
            if s == 1:
                put(sh, ch, sy.at[4 + i], intra)
            put(sh, ch, sx.at[0, s, i], xr)
            put(sh, ch, sx.at[1, s, i], xl)
            put(sh, ch, ssib.at[s, i], sib)

    def x_round(s):
        for i in range(2):
            for side, dx in ((0, 3), (1, 1)):
                sh, ch = shard(s, dx), mine[i]
                wait_w(sh, ch)
                if i == side:
                    put(sh, ch, sx.at[side, s, 2], xr if side == 0 else xl)
                put(sh, ch, ssib.at[s, 2 + 2 * side + i], sib)

    def far_round(s):
        for i in range(2):
            sh, ch = shard(s, 2), mine[i]
            wait_w(sh, ch)
            put(sh, ch, ssib.at[s, 6 + i], sib)

    def sib_round(s):
        for dx in range(4):
            if s == 0 and dx == 0:
                continue
            for i in range(2):
                wait_w(shard(s, dx), theirs[i])

    last_z = ~(wrap_lo | wrap_hi) & ((p // 2) % (HALF_SEQ // 2) == HALF_SEQ // 2 - 1)
    kinds = [kind.astype(jnp.int32) for kind in (~(wrap_lo | wrap_hi | last_z), wrap_hi, last_z, wrap_lo)]

    def run(fn, *spans):
        lo = sum(kind * span[0] for kind, span in zip(kinds, spans))
        hi = sum(kind * span[1] for kind, span in zip(kinds, spans))
        lax.fori_loop(lo, hi, fn, 0)

    def halo_if(cond, i):
        @pl.when(cond)
        def _():
            wait_halo((i,))

    none = (0, 0)
    leave = ((p // 2 == HALF_SEQ // 2) & ~wrap_hi).astype(jnp.int32)
    y_round(1)

    @pl.when(wrap_hi)
    def _():
        for i in range(3):
            to_relay(i).start()

    x_round(0)
    y_round(2)
    x_round(1)
    for copy in loads:
        copy.wait()
    usual = ~(wrap_hi | last_z | wrap_lo)
    halo_if(usual, 0)
    run(early, (0, 4), none, none, none)
    pass_on(0)
    y_round(3)
    far_round(0)
    pass_on(1)
    halo_if(wrap_lo, 0)
    run(early, (4, 8), none, none, (0, 8))
    own_w.wait()
    sib_round(0)
    halo_if(usual, 1)
    run(own_head, (0, 2), none, none, none)
    x_round(2)
    far_round(1)
    pass_on(2)
    sib_round(1)
    halo_if(wrap_hi, 0)
    run(early, none, (0, 8), none, none)
    x_round(3)
    far_round(2)
    halo_if(usual, 2)
    halo_if(wrap_hi | wrap_lo, 1)

    @pl.when(wrap_hi)
    def _():
        pl.semaphore_wait(ready, 1)

    run(own_head, (2, 4), (0, 4), none, (0, 4))
    sib_round(2)
    far_round(3)
    halo_if(last_z, 0)
    halo_if(last_z, 1)
    run(early, none, none, (0, 8), none)
    run(own_head, (4, 6), (4, 6), (0, 6), (4, 6))
    halo_if(~usual, 2)
    run(far_head, (0, 4 * (1 - leave)), none, none, none)
    sib_round(3)
    run(own_head, (6, 8), (6, 8), (6, 8), (6, 8))
    run(far_head, (4 * (1 - leave), 8), (0, 8), (0, 8), (0, 8))

    for c in pending:
        c.wait_send()
    for part in halo_parts:
        halo(*part, 1 - core, sib).wait_send()

    @pl.when(has_z)
    def _():
        for part in halo_parts:
            halo(*part, core, zdev).wait_send()

    @pl.when(relays)
    def _():
        for i in range(3):
            relay(i).wait_send()

    def drain(h, carry):
        for copy in send_d(h, 1 - core, sib):
            copy.wait_send()

        @pl.when(has_z)
        def _():
            for copy in send_d(h, core, zdev):
                copy.wait_send()

        return carry

    lax.fori_loop(0, HEADS, drain, 0)


def write_out(dq, dk, dv, dq_out, dk_out, dv_out, held, sem_in, sem_out):
    half = TOK // 2
    steps = []
    for i, (src, dst) in enumerate(((dq, dq_out), (dk, dk_out), (dv, dv_out))):
        for j in range(2):
            rows = pl.ds(j * half, half)
            n = 2 * i + j
            steps.append((
                pltpu.make_async_copy(src.at[0, rows], held.at[i, rows], sem_in.at[n]),
                pltpu.make_async_copy(held.at[i, rows], dst.at[0, rows], sem_out.at[n]),
            ))
    for first, _ in steps:
        first.start()
    for first, second in steps:
        first.wait()
        second.start()
    for _, second in steps:
        second.wait()


def body(queries, keys, values, d_out, w_out, pattern, valid):
    tok, width = queries.shape[1], queries.shape[2]
    vm = pl.BlockSpec(memory_space=pltpu.VMEM)
    sm = pl.BlockSpec(memory_space=pltpu.SMEM)
    hbm = pl.BlockSpec(memory_space=pltpu.HBM)
    out = jax.ShapeDtypeStruct((1, tok, width), BF)
    dma = pltpu.SemaphoreType.DMA
    grads = pl.pallas_call(
        kernel,
        out_shape=(out, out, out),
        in_specs=[sm, sm, hbm, hbm, hbm, hbm, hbm],
        out_specs=(vm, vm, vm),
        scratch_shapes=[
            pltpu.VMEM((3, tok, width), BF),
            pltpu.VMEM((3, tok, width), BF),
            pltpu.VMEM((3, tok, width), BF),
            pltpu.VMEM((tok, D), BF),
            pltpu.VMEM((16, 4, 16, D), BF),
            pltpu.VMEM((2, HEADS, tok, HD), BF),
            pltpu.VMEM((2, HEADS, 8, 128), F32),
            pltpu.VMEM((HEADS, tok, HD), BF),
            pltpu.VMEM((HEADS, 8, 128), F32),
            pltpu.VMEM((HEADS, 3 * tok, tok), F32),
            pltpu.VMEM((HEADS, tok, HD), F32),
            pltpu.VMEM((HEADS, tok, HD), F32),
            pltpu.VMEM((3, tok, width), BF),
            dma((16, 4)),
            dma((2, 4, 3)),
            dma((6,)),
            dma((4, 8)),
            dma((2, 3)),
            dma((2, 3)),
            dma((2, HEADS)),
            dma((2, HEADS)),
            dma((2, HEADS)),
            dma((2, HEADS)),
            dma,
            dma((4,)),
            pltpu.SemaphoreType.REGULAR,
            dma((3,)),
        ],
        compiler_params=pltpu.CompilerParams(
            collective_id=0, has_side_effects=True
        ),
        name="attention_backward",
    )(pattern.T, valid, queries, keys, values, d_out, w_out.reshape(4, 16, D))
    hb = pl.BlockSpec(memory_space=pl.ANY)
    return pl.pallas_call(
        write_out,
        out_shape=(out, out, out),
        in_specs=[hb, hb, hb],
        out_specs=(hb, hb, hb),
        scratch_shapes=[pltpu.VMEM((3, tok, width), BF), dma((6,)), dma((6,))],
        name="write_out",
    )(*grads)


def solution(mesh):
    spec = P("fsdp", "seq", None)
    in_specs = (spec, spec, spec, spec, P("fsdp", None), P(), P("fsdp", None))
    return jax.shard_map(
        body, mesh=mesh, in_specs=in_specs, out_specs=(spec, spec, spec), check_vma=False
    )
```

```python
import functools

import jax
import jax.numpy as jnp
from jax import lax
from jax.experimental import pallas as pl
from jax.experimental.pallas import tpu as pltpu
from jax.sharding import PartitionSpec as P

HEADS = 8
HD = 128
TOK = 128
N_SEQ = 48
HALF_SEQ = 24
D = 2048
SCALE = HD ** (-0.5)
MESH = pl.DeviceIdType.MESH
ORDER = (0, 1, 3, 2)
BF = jnp.bfloat16
F32 = jnp.float32


def nt(a, b):
    return lax.dot_general(a, b, (((1,), (1,)), ((), ())), preferred_element_type=F32)


def tn(a, b):
    return lax.dot_general(a, b, (((0,), (0,)), ((), ())), preferred_element_type=F32)


def nn(a, b):
    return lax.dot_general(a, b, (((1,), (0,)), ((), ())), preferred_element_type=F32)


def kernel(
    pat_ref, val_ref, q_hbm, k_hbm, v_hbm, do_hbm, w_ref,
    dq_ref, dk_ref, dv_ref,
    qb, kb, vb, do_ref, wf, dh, sth, d_own, st_own, prob, dk_acc, dv_acc, rel,
    wr, sx, sy, ssib, hs_s, hs_r, ds_s, ds_r, ts_s, ts_r, lsem, isem, ready, rel_r,
):
    p = lax.axis_index("seq")
    f = lax.axis_index("fsdp")
    core = p % 2
    low = p // HALF_SEQ
    k_y = f // 4
    x = f % 4
    sgn = 2 * low - 1
    sib = (p + 1 - 2 * core, f)
    zdev = (p - 1 + 2 * core, f)
    other_y = p + HALF_SEQ * (1 - 2 * low)
    xr = (p, k_y * 4 + (x + 1) % 4)
    xl = (p, k_y * 4 + (x + 3) % 4)
    inter = (other_y, ((k_y + sgn + 4) % 4) * 4 + x)
    intra = (other_y, f)
    opp = (other_y, ((k_y + 2) % 4) * 4 + x)
    has_l = p > 0
    has_r = p < N_SEQ - 1
    has_z = has_l & has_r
    wrap_lo = p == HALF_SEQ - 1
    wrap_hi = p == HALF_SEQ
    relays = p == 0
    wrap_dev = (HALF_SEQ - 1, f)
    greets_last = has_z & (((core == 0) & (p != HALF_SEQ)) | wrap_lo)
    greets_first = has_z & (((core == 1) & (p != HALF_SEQ - 1)) | wrap_hi)

    loads = [
        pltpu.make_async_copy(a, b, isem.at[i])
        for i, (a, b) in enumerate(
            (
                (k_hbm.at[0], kb.at[1]),
                (q_hbm.at[0], qb.at[1]),
                (v_hbm.at[0], vb.at[1]),
                (do_hbm.at[0], do_ref),
            )
        )
    ]
    own_w = pltpu.make_async_copy(w_ref, wf.at[f], lsem)
    for copy in loads:
        copy.start()
    own_w.start()

    barrier = pltpu.get_barrier_semaphore()
    for dev in (sib, xr, xl, inter, intra, opp):
        pl.semaphore_signal(barrier, inc=1, device_id=dev, device_id_type=MESH)

    @pl.when(greets_first)
    def _():
        pl.semaphore_signal(barrier, inc=1, device_id=zdev, device_id_type=MESH)

    @pl.when(relays)
    def _():
        pl.semaphore_signal(barrier, inc=1, device_id=wrap_dev, device_id_type=MESH)

    @pl.when(greets_last & ~wrap_lo)
    def _():
        pl.semaphore_wait(barrier, 7)
        pl.semaphore_signal(ready, inc=1, device_id=zdev, device_id_type=MESH)

    @pl.when(wrap_lo)
    def _():
        pl.semaphore_wait(barrier, 8)
        for dev in (zdev, (0, f)):
            pl.semaphore_signal(ready, inc=1, device_id=dev, device_id_type=MESH)

    @pl.when(~greets_last)
    def _():
        pl.semaphore_wait(barrier, 6)

    def rcopy(src, dst, ssem, rsem, dev):
        return pltpu.make_async_remote_copy(
            src_ref=src, dst_ref=dst, send_sem=ssem, recv_sem=rsem,
            device_id=dev, device_id_type=MESH,
        )

    pending = []

    def put_own(ch, ssem, dev):
        c = rcopy(w_ref.at[ch], wf.at[f, ch], ssem, wr.at[f, ch], dev)
        c.start()
        pending.append(c)

    def put(sh, ch, ssem, dev):
        c = rcopy(wf.at[sh, ch], wf.at[sh, ch], ssem, wr.at[sh, ch], dev)
        c.start()
        pending.append(c)

    def pair(sh, row, ssem):
        rows = wf.at[sh, pl.ds(row, 2)]
        return rcopy(rows, rows, ssem, wr.at[sh, row], sib)

    def put_pair(sh, ssem):
        c = pair(sh, 2 * core, ssem)
        c.start()
        pending.append(c)

    def wait_w(sh, ch):
        rcopy(wf.at[sh, ch], wf.at[sh, ch], lsem, wr.at[sh, ch], sib).wait_recv()

    def shard(s, dx):
        return ((k_y + sgn * ORDER[s] + 4) % 4) * 4 + (x + dx) % 4

    mine = (2 * core, 2 * core + 1)

    for i in range(2):
        put_own(mine[i], sy.at[i], inter)
        put_own(mine[i], sx.at[0, 0, i], xr)
        put_own(mine[i], sx.at[1, 0, i], xl)
    for i in range(2):
        put_own(mine[i], sy.at[2 + i], opp)

    halo_parts = ((0, k_hbm, kb), (1, v_hbm, vb), (2, q_hbm, qb))

    def halo(i, src, dst, side, dev):
        return rcopy(
            src.at[0], dst.at[2 - 2 * side], hs_s.at[side, i], hs_r.at[1 - side, i], dev
        )

    def halo_to(side, dev):
        for i, src, dst in halo_parts:
            halo(i, src, dst, side, dev).start()

    halo_to(1 - core, sib)

    @pl.when(greets_last)
    def _():
        halo_to(core, zdev)

    @pl.when(greets_first & (p != HALF_SEQ))
    def _():
        pl.semaphore_wait(ready, 1)
        halo_to(core, zdev)

    def to_relay(i):
        return rcopy(halo_parts[i][1].at[0], rel.at[i], hs_s.at[0, i], rel_r.at[i], intra)

    def relay(i):
        dst = halo_parts[i][2].at[2]
        return rcopy(rel.at[i], dst, hs_s.at[0, i], hs_r.at[1, i], wrap_dev)

    def pass_on(i):
        @pl.when(relays)
        def _():
            if i == 0:
                pl.semaphore_wait(ready, 1)
            to_relay(i).wait_recv()
            relay(i).start()

    def wait_halo(which):
        for i in which:
            halo(*halo_parts[i], core, sib).wait_recv()

        @pl.when(has_z)
        def _():
            for i in which:
                halo(*halo_parts[i], 1 - core, sib).wait_recv()

    @pl.when(~has_z)
    def _():
        for buf in (kb, vb, qb):
            buf[2 * core] = jnp.zeros((TOK, HEADS * HD), BF)
        dh[core] = jnp.zeros((HEADS, TOK, HD), BF)
        sth[core] = jnp.zeros((HEADS, 8, 128), F32)

    def limit(qblock, kblock, ok):
        row = (qblock + N_SEQ) % N_SEQ
        hit = pat_ref[0, row] == kblock
        for i in range(1, 4):
            hit = hit | (pat_ref[i, row] == kblock)
        return jnp.where(hit & ok, val_ref[0, (kblock + N_SEQ) % N_SEQ], 0)

    lim_own = (limit(p, p - 1, has_l), limit(p, p, p >= 0), limit(p, p + 1, has_r))
    lim_far = (limit(p - 1, p, has_l), limit(p + 1, p, has_r))

    def masked(score, lim):
        rows = lax.broadcasted_iota(jnp.int32, (TOK, TOK), 0)
        return jnp.where(rows < lim, score * SCALE, -jnp.inf)

    def head_of(t):
        s = t // 2
        turn = s + (s // 2) * (1 - 2 * (s % 2))
        return ((k_y + sgn * turn + 4) % 4) * 2 + (x // 2 + t) % 2

    def lanes(h):
        return pl.ds(pl.multiple_of(h * HD, HD), HD)

    def thirds(a):
        return a[:TOK], a[TOK : 2 * TOK], a[2 * TOK :]

    def early(t, carry):
        h = head_of(t)
        c = lanes(h)
        score = nt(kb[:, :, c].reshape(3 * TOK, HD), qb[1, :, c])
        s0, s1, s2 = (masked(a, lim) for a, lim in zip(thirds(score), lim_own))
        top = jnp.max(jnp.maximum(jnp.maximum(s0, s1), s2), axis=0, keepdims=True)
        e0, e1, e2 = jnp.exp(s0 - top), jnp.exp(s1 - top), jnp.exp(s2 - top)
        total = jnp.sum(e0 + e1 + e2, axis=0, keepdims=True)
        inv = 1.0 / total
        prob[h, 0:TOK] = e0 * inv
        prob[h, TOK : 2 * TOK] = e1 * inv
        prob[h, 2 * TOK :] = e2 * inv
        st_own[h, 0:1, :] = top + jnp.log(total)
        return carry

    def send_d(h, side, dev):
        return (
            rcopy(d_own.at[h], dh.at[1 - side, h], ds_s.at[side, h], ds_r.at[1 - side, h], dev),
            rcopy(st_own.at[h], sth.at[1 - side, h], ts_s.at[side, h], ts_r.at[1 - side, h], dev),
        )

    def own_head(t, carry):
        h = head_of(t)
        c = lanes(h)
        w_h = wf[pl.ds(2 * h, 2)].reshape(HD, D)
        d = nt(do_ref[...], w_h).astype(BF)
        d_own[h] = d
        dp = nt(vb[:, :, c].reshape(3 * TOK, HD), d)
        pr = prob[h]
        prb = pr.astype(BF)
        delta = jnp.sum(prb.astype(F32) * dp, axis=0, keepdims=True)
        st_own[h, 1:2, :] = delta

        @pl.when(has_z)
        def _():
            for copy in send_d(h, core, zdev):
                copy.start()

        for copy in send_d(h, 1 - core, sib):
            copy.start()
        ds = (pr * (dp - delta)).astype(BF)
        dq = tn(ds, kb[:, :, c].reshape(3 * TOK, HD))
        dq_ref[0, :, c] = (dq * SCALE).astype(BF)
        dk_acc[h] = nn(ds[TOK : 2 * TOK], qb[1, :, c])
        dv_acc[h] = nn(prb[TOK : 2 * TOK], d)
        return carry

    def far_head(t, carry):
        h = head_of(t)
        c = lanes(h)
        for copy in send_d(h, core, sib):
            copy.wait_recv()

        @pl.when(has_z)
        def _():
            for copy in send_d(h, 1 - core, sib):
                copy.wait_recv()

        q = jnp.concatenate([qb[0, :, c], qb[2, :, c]], axis=0)
        d = dh[:, h].reshape(2 * TOK, HD)
        score = nt(kb[1, :, c], q)
        dp = nt(vb[1, :, c], d)
        pr, ds = [], []
        for side in range(2):
            cols = slice(side * TOK, (side + 1) * TOK)
            a = jnp.exp(masked(score[:, cols], lim_far[side]) - sth[side, h, 0:1, :])
            pr.append(a.astype(BF))
            ds.append((a * (dp[:, cols] - sth[side, h, 1:2, :])).astype(BF))
        dk = dk_acc[h] + nn(jnp.concatenate(ds, axis=1), q)
        dv = dv_acc[h] + nn(jnp.concatenate(pr, axis=1), d)
        dk_ref[0, :, c] = (dk * SCALE).astype(BF)
        dv_ref[0, :, c] = dv.astype(BF)
        return carry

    def y_round(s):
        for i in range(2):
            sh, ch = shard(s, 0), mine[i]
            wait_w(sh, ch)
            if s == 1:
                put(sh, ch, sy.at[4 + i], intra)
            put(sh, ch, sx.at[0, s, i], xr)
            put(sh, ch, sx.at[1, s, i], xl)
        put_pair(shard(s, 0), ssib.at[s, 0])

    def x_round(s):
        for i in range(2):
            for side, dx in ((0, 3), (1, 1)):
                sh, ch = shard(s, dx), mine[i]
                wait_w(sh, ch)
                if i == side:
                    put(sh, ch, sx.at[side, s, 2], xr if side == 0 else xl)
        put_pair(shard(s, 3), ssib.at[s, 1])
        put_pair(shard(s, 1), ssib.at[s, 2])

    def far_round(s):
        for i in range(2):
            wait_w(shard(s, 2), mine[i])
        put_pair(shard(s, 2), ssib.at[s, 3])

    def sib_round(s):
        for dx in range(4):
            if s == 0 and dx == 0:
                continue
            pair(shard(s, dx), 2 - 2 * core, lsem).wait_recv()

    last_z = ~(wrap_lo | wrap_hi) & ((p // 2) % (HALF_SEQ // 2) == HALF_SEQ // 2 - 1)
    kinds = [kind.astype(jnp.int32) for kind in (~(wrap_lo | wrap_hi | last_z), wrap_hi, last_z, wrap_lo)]

    def run(fn, *spans):
        lo = sum(kind * span[0] for kind, span in zip(kinds, spans))
        hi = sum(kind * span[1] for kind, span in zip(kinds, spans))
        lax.fori_loop(lo, hi, fn, 0)

    def halo_if(cond, i):
        @pl.when(cond)
        def _():
            wait_halo((i,))

    none = (0, 0)
    leave = ((p // 2 == HALF_SEQ // 2) & ~wrap_hi).astype(jnp.int32)
    y_round(1)

    @pl.when(wrap_hi)
    def _():
        for i in range(3):
            to_relay(i).start()

    x_round(0)
    y_round(2)
    x_round(1)
    for copy in loads:
        copy.wait()
    usual = ~(wrap_hi | last_z | wrap_lo)
    halo_if(usual, 0)
    run(early, (0, 4), none, none, none)
    pass_on(0)
    y_round(3)
    far_round(0)
    pass_on(1)
    halo_if(wrap_lo, 0)
    run(early, (4, 8), none, none, (0, 8))
    own_w.wait()
    sib_round(0)
    halo_if(usual, 1)
    run(own_head, (0, 2), none, none, none)
    x_round(2)
    far_round(1)
    pass_on(2)
    sib_round(1)
    halo_if(wrap_hi, 0)
    run(early, none, (0, 8), none, none)
    x_round(3)
    far_round(2)
    halo_if(usual, 2)
    halo_if(wrap_hi | wrap_lo, 1)

    @pl.when(wrap_hi)
    def _():
        pl.semaphore_wait(ready, 1)

    run(own_head, (2, 4), (0, 4), none, (0, 4))
    sib_round(2)
    far_round(3)
    halo_if(last_z, 0)
    halo_if(last_z, 1)
    run(early, none, none, (0, 8), none)
    run(own_head, (4, 6), (4, 6), (0, 6), (4, 6))
    halo_if(~usual, 2)
    run(far_head, (0, 4 * (1 - leave)), none, none, none)
    sib_round(3)
    run(own_head, (6, 8), (6, 8), (6, 8), (6, 8))
    run(far_head, (4 * (1 - leave), 8), (0, 8), (0, 8), (0, 8))

    for c in pending:
        c.wait_send()
    for part in halo_parts:
        halo(*part, 1 - core, sib).wait_send()

    @pl.when(has_z)
    def _():
        for part in halo_parts:
            halo(*part, core, zdev).wait_send()

    @pl.when(relays)
    def _():
        for i in range(3):
            relay(i).wait_send()

    def drain(h, carry):
        for copy in send_d(h, 1 - core, sib):
            copy.wait_send()

        @pl.when(has_z)
        def _():
            for copy in send_d(h, core, zdev):
                copy.wait_send()

        return carry

    lax.fori_loop(0, HEADS, drain, 0)


def write_out(dq, dk, dv, dq_out, dk_out, dv_out, held, sem_in, sem_out):
    half = TOK // 2
    steps = []
    for i, (src, dst) in enumerate(((dq, dq_out), (dk, dk_out), (dv, dv_out))):
        for j in range(2):
            rows = pl.ds(j * half, half)
            n = 2 * i + j
            steps.append((
                pltpu.make_async_copy(src.at[0, rows], held.at[i, rows], sem_in.at[n]),
                pltpu.make_async_copy(held.at[i, rows], dst.at[0, rows], sem_out.at[n]),
            ))
    for first, _ in steps:
        first.start()
    for first, second in steps:
        first.wait()
        second.start()
    for _, second in steps:
        second.wait()


def body(queries, keys, values, d_out, w_out, pattern, valid):
    tok, width = queries.shape[1], queries.shape[2]
    vm = pl.BlockSpec(memory_space=pltpu.VMEM)
    sm = pl.BlockSpec(memory_space=pltpu.SMEM)
    hbm = pl.BlockSpec(memory_space=pltpu.HBM)
    out = jax.ShapeDtypeStruct((1, tok, width), BF)
    dma = pltpu.SemaphoreType.DMA
    grads = pl.pallas_call(
        kernel,
        out_shape=(out, out, out),
        in_specs=[sm, sm, hbm, hbm, hbm, hbm, hbm],
        out_specs=(vm, vm, vm),
        scratch_shapes=[
            pltpu.VMEM((3, tok, width), BF),
            pltpu.VMEM((3, tok, width), BF),
            pltpu.VMEM((3, tok, width), BF),
            pltpu.VMEM((tok, D), BF),
            pltpu.VMEM((16, 4, 16, D), BF),
            pltpu.VMEM((2, HEADS, tok, HD), BF),
            pltpu.VMEM((2, HEADS, 8, 128), F32),
            pltpu.VMEM((HEADS, tok, HD), BF),
            pltpu.VMEM((HEADS, 8, 128), F32),
            pltpu.VMEM((HEADS, 3 * tok, tok), F32),
            pltpu.VMEM((HEADS, tok, HD), F32),
            pltpu.VMEM((HEADS, tok, HD), F32),
            pltpu.VMEM((3, tok, width), BF),
            dma((16, 4)),
            dma((2, 4, 3)),
            dma((6,)),
            dma((4, 4)),
            dma((2, 3)),
            dma((2, 3)),
            dma((2, HEADS)),
            dma((2, HEADS)),
            dma((2, HEADS)),
            dma((2, HEADS)),
            dma,
            dma((4,)),
            pltpu.SemaphoreType.REGULAR,
            dma((3,)),
        ],
        compiler_params=pltpu.CompilerParams(
            collective_id=0, has_side_effects=True
        ),
        name="attention_backward",
    )(pattern.T, valid, queries, keys, values, d_out, w_out.reshape(4, 16, D))
    hb = pl.BlockSpec(memory_space=pl.ANY)
    return pl.pallas_call(
        write_out,
        out_shape=(out, out, out),
        in_specs=[hb, hb, hb],
        out_specs=(hb, hb, hb),
        scratch_shapes=[pltpu.VMEM((3, tok, width), BF), dma((6,)), dma((6,))],
        name="write_out",
    )(*grads)


def solution(mesh):
    spec = P("fsdp", "seq", None)
    in_specs = (spec, spec, spec, spec, P("fsdp", None), P(), P("fsdp", None))
    return jax.shard_map(
        body, mesh=mesh, in_specs=in_specs, out_specs=(spec, spec, spec), check_vma=False
    )
```

```python
import functools

import jax
import jax.numpy as jnp
from jax import lax
from jax.experimental import pallas as pl
from jax.experimental.pallas import tpu as pltpu
from jax.sharding import PartitionSpec as P

HEADS = 8
HD = 128
TOK = 128
N_SEQ = 48
HALF_SEQ = 24
D = 2048
SCALE = HD ** (-0.5)
MESH = pl.DeviceIdType.MESH
ORDER = (0, 1, 3, 2)
BF = jnp.bfloat16
F32 = jnp.float32


def nt(a, b):
    return lax.dot_general(a, b, (((1,), (1,)), ((), ())), preferred_element_type=F32)


def tn(a, b):
    return lax.dot_general(a, b, (((0,), (0,)), ((), ())), preferred_element_type=F32)


def nn(a, b):
    return lax.dot_general(a, b, (((1,), (0,)), ((), ())), preferred_element_type=F32)


def kernel(
    pat_ref, val_ref, q_hbm, k_hbm, v_hbm, do_hbm, w_ref,
    dq_ref, dk_ref, dv_ref,
    qb, kb, vb, do_ref, wf, dh, sth, d_own, st_own, prob, dk_acc, dv_acc, rel,
    wr, sx, sy, ssib, hs_s, hs_r, ds_s, ds_r, ts_s, ts_r, lsem, isem, ready, rel_r,
):
    p = lax.axis_index("seq")
    f = lax.axis_index("fsdp")
    core = p % 2
    low = p // HALF_SEQ
    k_y = f // 4
    x = f % 4
    sgn = 2 * low - 1
    sib = (p + 1 - 2 * core, f)
    zdev = (p - 1 + 2 * core, f)
    other_y = p + HALF_SEQ * (1 - 2 * low)
    xr = (p, k_y * 4 + (x + 1) % 4)
    xl = (p, k_y * 4 + (x + 3) % 4)
    inter = (other_y, ((k_y + sgn + 4) % 4) * 4 + x)
    intra = (other_y, f)
    opp = (other_y, ((k_y + 2) % 4) * 4 + x)
    has_l = p > 0
    has_r = p < N_SEQ - 1
    has_z = has_l & has_r
    wrap_lo = p == HALF_SEQ - 1
    wrap_hi = p == HALF_SEQ
    relays = p == 0
    wrap_dev = (HALF_SEQ - 1, f)
    greets_last = has_z & (((core == 0) & (p != HALF_SEQ)) | wrap_lo)
    greets_first = has_z & (((core == 1) & (p != HALF_SEQ - 1)) | wrap_hi)

    loads = [
        pltpu.make_async_copy(a, b, isem.at[i])
        for i, (a, b) in enumerate(
            (
                (k_hbm.at[0], kb.at[1]),
                (q_hbm.at[0], qb.at[1]),
                (v_hbm.at[0], vb.at[1]),
                (do_hbm.at[0], do_ref),
            )
        )
    ]
    own_w = pltpu.make_async_copy(w_ref, wf.at[f], lsem)
    for copy in loads:
        copy.start()
    own_w.start()

    barrier = pltpu.get_barrier_semaphore()
    for dev in (sib, xr, xl, inter, intra, opp):
        pl.semaphore_signal(barrier, inc=1, device_id=dev, device_id_type=MESH)

    @pl.when(greets_first)
    def _():
        pl.semaphore_signal(barrier, inc=1, device_id=zdev, device_id_type=MESH)

    @pl.when(relays)
    def _():
        pl.semaphore_signal(barrier, inc=1, device_id=wrap_dev, device_id_type=MESH)

    @pl.when(greets_last & ~wrap_lo)
    def _():
        pl.semaphore_wait(barrier, 7)
        pl.semaphore_signal(ready, inc=1, device_id=zdev, device_id_type=MESH)

    @pl.when(wrap_lo)
    def _():
        pl.semaphore_wait(barrier, 8)
        for dev in (zdev, (0, f)):
            pl.semaphore_signal(ready, inc=1, device_id=dev, device_id_type=MESH)

    @pl.when(~greets_last)
    def _():
        pl.semaphore_wait(barrier, 6)

    def rcopy(src, dst, ssem, rsem, dev):
        return pltpu.make_async_remote_copy(
            src_ref=src, dst_ref=dst, send_sem=ssem, recv_sem=rsem,
            device_id=dev, device_id_type=MESH,
        )

    pending = []

    def put_own(ch, ssem, dev):
        c = rcopy(w_ref.at[ch], wf.at[f, ch], ssem, wr.at[f, ch], dev)
        c.start()
        pending.append(c)

    def put(sh, ch, ssem, dev):
        c = rcopy(wf.at[sh, ch], wf.at[sh, ch], ssem, wr.at[sh, ch], dev)
        c.start()
        pending.append(c)

    def pair(sh, row, ssem):
        rows = wf.at[sh, pl.ds(row, 2)]
        return rcopy(rows, rows, ssem, wr.at[sh, row], sib)

    def put_pair(sh, ssem):
        c = pair(sh, 2 * core, ssem)
        c.start()
        pending.append(c)

    def wait_w(sh, ch):
        rcopy(wf.at[sh, ch], wf.at[sh, ch], lsem, wr.at[sh, ch], sib).wait_recv()

    def shard(s, dx):
        return ((k_y + sgn * ORDER[s] + 4) % 4) * 4 + (x + dx) % 4

    mine = (2 * core, 2 * core + 1)

    for i in range(2):
        put_own(mine[i], sy.at[i], inter)
        put_own(mine[i], sx.at[0, 0, i], xr)
        put_own(mine[i], sx.at[1, 0, i], xl)
    for i in range(2):
        put_own(mine[i], sy.at[2 + i], opp)

    halo_parts = ((0, k_hbm, kb), (1, v_hbm, vb), (2, q_hbm, qb))

    def halo(i, src, dst, side, dev):
        return rcopy(
            src.at[0], dst.at[2 - 2 * side], hs_s.at[side, i], hs_r.at[1 - side, i], dev
        )

    def halo_to(side, dev):
        for i, src, dst in halo_parts:
            halo(i, src, dst, side, dev).start()

    halo_to(1 - core, sib)

    @pl.when(greets_last)
    def _():
        halo_to(core, zdev)

    @pl.when(greets_first & (p != HALF_SEQ))
    def _():
        pl.semaphore_wait(ready, 1)
        halo_to(core, zdev)

    def to_relay(i):
        return rcopy(halo_parts[i][1].at[0], rel.at[i], hs_s.at[0, i], rel_r.at[i], intra)

    def relay(i):
        dst = halo_parts[i][2].at[2]
        return rcopy(rel.at[i], dst, hs_s.at[0, i], hs_r.at[1, i], wrap_dev)

    def pass_on(i):
        @pl.when(relays)
        def _():
            if i == 0:
                pl.semaphore_wait(ready, 1)
            to_relay(i).wait_recv()
            relay(i).start()

    def wait_halo(which):
        for i in which:
            halo(*halo_parts[i], core, sib).wait_recv()

        @pl.when(has_z)
        def _():
            for i in which:
                halo(*halo_parts[i], 1 - core, sib).wait_recv()

    @pl.when(~has_z)
    def _():
        for buf in (kb, vb, qb):
            buf[2 * core] = jnp.zeros((TOK, HEADS * HD), BF)
        dh[core] = jnp.zeros((HEADS, TOK, HD), BF)
        sth[core] = jnp.zeros((HEADS, 8, 128), F32)

    def limit(qblock, kblock, ok):
        row = (qblock + N_SEQ) % N_SEQ
        hit = pat_ref[0, row] == kblock
        for i in range(1, 4):
            hit = hit | (pat_ref[i, row] == kblock)
        return jnp.where(hit & ok, val_ref[0, (kblock + N_SEQ) % N_SEQ], 0)

    lim_own = (limit(p, p - 1, has_l), limit(p, p, p >= 0), limit(p, p + 1, has_r))
    lim_far = (limit(p - 1, p, has_l), limit(p + 1, p, has_r))

    def masked(score, lim):
        rows = lax.broadcasted_iota(jnp.int32, (TOK, TOK), 0)
        return jnp.where(rows < lim, score * SCALE, -jnp.inf)

    def head_of(t):
        s = t // 2
        turn = s + (s // 2) * (1 - 2 * (s % 2))
        return ((k_y + sgn * turn + 4) % 4) * 2 + (x // 2 + t) % 2

    def lanes(h):
        return pl.ds(pl.multiple_of(h * HD, HD), HD)

    def thirds(a):
        return a[:TOK], a[TOK : 2 * TOK], a[2 * TOK :]

    def early(t, carry):
        h = head_of(t)
        c = lanes(h)
        score = nt(kb[:, :, c].reshape(3 * TOK, HD), qb[1, :, c])
        s0, s1, s2 = (masked(a, lim) for a, lim in zip(thirds(score), lim_own))
        top = jnp.max(jnp.maximum(jnp.maximum(s0, s1), s2), axis=0, keepdims=True)
        e0, e1, e2 = jnp.exp(s0 - top), jnp.exp(s1 - top), jnp.exp(s2 - top)
        total = jnp.sum(e0 + e1 + e2, axis=0, keepdims=True)
        inv = 1.0 / total
        prob[h, 0:TOK] = e0 * inv
        prob[h, TOK : 2 * TOK] = e1 * inv
        prob[h, 2 * TOK :] = e2 * inv
        st_own[h, 0:1, :] = top + jnp.log(total)
        return carry

    def send_d(h, side, dev):
        return (
            rcopy(d_own.at[h], dh.at[1 - side, h], ds_s.at[side, h], ds_r.at[1 - side, h], dev),
            rcopy(st_own.at[h], sth.at[1 - side, h], ts_s.at[side, h], ts_r.at[1 - side, h], dev),
        )

    def own_head(t, carry):
        h = head_of(t)
        c = lanes(h)
        w_h = wf[pl.ds(2 * h, 2)].reshape(HD, D)
        d = nt(do_ref[...], w_h).astype(BF)
        d_own[h] = d
        dp = nt(vb[:, :, c].reshape(3 * TOK, HD), d)
        pr = prob[h]
        prb = pr.astype(BF)
        delta = jnp.sum(prb.astype(F32) * dp, axis=0, keepdims=True)
        st_own[h, 1:2, :] = delta

        @pl.when(has_z)
        def _():
            for copy in send_d(h, core, zdev):
                copy.start()

        for copy in send_d(h, 1 - core, sib):
            copy.start()
        ds = (pr * (dp - delta)).astype(BF)
        dq = tn(ds, kb[:, :, c].reshape(3 * TOK, HD))
        dq_ref[0, :, c] = (dq * SCALE).astype(BF)
        dk_acc[h] = nn(ds[TOK : 2 * TOK], qb[1, :, c])
        dv_acc[h] = nn(prb[TOK : 2 * TOK], d)
        return carry

    def far_head(t, carry):
        h = head_of(t)
        c = lanes(h)
        for copy in send_d(h, core, sib):
            copy.wait_recv()

        @pl.when(has_z)
        def _():
            for copy in send_d(h, 1 - core, sib):
                copy.wait_recv()

        q = jnp.concatenate([qb[0, :, c], qb[2, :, c]], axis=0)
        d = dh[:, h].reshape(2 * TOK, HD)
        score = nt(kb[1, :, c], q)
        dp = nt(vb[1, :, c], d)
        pr, ds = [], []
        for side in range(2):
            cols = slice(side * TOK, (side + 1) * TOK)
            a = jnp.exp(masked(score[:, cols], lim_far[side]) - sth[side, h, 0:1, :])
            pr.append(a.astype(BF))
            ds.append((a * (dp[:, cols] - sth[side, h, 1:2, :])).astype(BF))
        dk = dk_acc[h] + nn(jnp.concatenate(ds, axis=1), q)
        dv = dv_acc[h] + nn(jnp.concatenate(pr, axis=1), d)
        dk_ref[0, :, c] = (dk * SCALE).astype(BF)
        dv_ref[0, :, c] = dv.astype(BF)
        return carry

    def y_round(s):
        for i in range(2):
            sh, ch = shard(s, 0), mine[i]
            wait_w(sh, ch)
            if s == 1:
                put(sh, ch, sy.at[4 + i], intra)
            put(sh, ch, sx.at[0, s, i], xr)
            put(sh, ch, sx.at[1, s, i], xl)
        put_pair(shard(s, 0), ssib.at[s, 0])

    def x_round(s):
        for i in range(2):
            for side, dx in ((0, 3), (1, 1)):
                sh, ch = shard(s, dx), mine[i]
                wait_w(sh, ch)
                if i == side:
                    put(sh, ch, sx.at[side, s, 2], xr if side == 0 else xl)
        put_pair(shard(s, 3), ssib.at[s, 1])
        put_pair(shard(s, 1), ssib.at[s, 2])

    def far_round(s):
        for i in range(2):
            wait_w(shard(s, 2), mine[i])
        put_pair(shard(s, 2), ssib.at[s, 3])

    def sib_round(s):
        for dx in range(4):
            if s == 0 and dx == 0:
                continue
            pair(shard(s, dx), 2 - 2 * core, lsem).wait_recv()

    last_z = ~(wrap_lo | wrap_hi) & ((p // 2) % (HALF_SEQ // 2) == HALF_SEQ // 2 - 1)
    kinds = [kind.astype(jnp.int32) for kind in (~(wrap_lo | wrap_hi | last_z), wrap_hi, last_z, wrap_lo)]

    def run(fn, *spans):
        lo = sum(kind * span[0] for kind, span in zip(kinds, spans))
        hi = sum(kind * span[1] for kind, span in zip(kinds, spans))
        lax.fori_loop(lo, hi, fn, 0)

    def halo_if(cond, i):
        @pl.when(cond)
        def _():
            wait_halo((i,))

    none = (0, 0)
    leave = ((p // 2 == HALF_SEQ // 2) & ~wrap_hi).astype(jnp.int32)
    y_round(1)

    @pl.when(wrap_hi)
    def _():
        for i in range(3):
            to_relay(i).start()

    x_round(0)
    y_round(2)
    x_round(1)
    for copy in loads:
        copy.wait()
    usual = ~(wrap_hi | last_z | wrap_lo)
    halo_if(usual, 0)
    run(early, (0, 4), none, none, none)
    pass_on(0)
    y_round(3)
    far_round(0)
    pass_on(1)
    halo_if(wrap_lo, 0)
    run(early, (4, 8), none, none, (0, 8))
    own_w.wait()
    sib_round(0)
    halo_if(usual, 1)
    run(own_head, (0, 2), none, none, none)
    x_round(2)
    far_round(1)
    pass_on(2)
    sib_round(1)
    halo_if(wrap_hi, 0)
    run(early, none, (0, 8), none, none)
    x_round(3)
    far_round(2)
    halo_if(usual, 2)
    halo_if(wrap_hi | wrap_lo, 1)

    @pl.when(wrap_hi)
    def _():
        pl.semaphore_wait(ready, 1)

    run(own_head, (2, 4), (0, 4), none, (0, 4))
    sib_round(2)
    far_round(3)
    halo_if(last_z, 0)
    halo_if(last_z, 1)
    run(early, none, none, (0, 8), none)
    run(own_head, (4, 6), (4, 6), (0, 6), (4, 6))
    halo_if(~usual, 2)
    run(far_head, (0, 4 * (1 - leave)), none, none, none)
    sib_round(3)
    run(own_head, (6, 8), (6, 8), (6, 8), (6, 8))
    run(far_head, (4 * (1 - leave), 8), (0, 8), (0, 8), (0, 8))

    for c in pending:
        c.wait_send()
    for part in halo_parts:
        halo(*part, 1 - core, sib).wait_send()

    @pl.when(has_z)
    def _():
        for part in halo_parts:
            halo(*part, core, zdev).wait_send()

    @pl.when(relays)
    def _():
        for i in range(3):
            relay(i).wait_send()

    def drain(h, carry):
        for copy in send_d(h, 1 - core, sib):
            copy.wait_send()

        @pl.when(has_z)
        def _():
            for copy in send_d(h, core, zdev):
                copy.wait_send()

        return carry

    lax.fori_loop(0, HEADS, drain, 0)


def write_out(dq, dk, dv, dq_out, dk_out, dv_out, held, sem_in, sem_out):
    part = TOK // 4
    steps = []
    for i, (src, dst) in enumerate(((dq, dq_out), (dk, dk_out), (dv, dv_out))):
        for j in range(4):
            rows = pl.ds(j * part, part)
            n = 4 * i + j
            steps.append((
                pltpu.make_async_copy(src.at[0, rows], held.at[i, rows], sem_in.at[n]),
                pltpu.make_async_copy(held.at[i, rows], dst.at[0, rows], sem_out.at[n]),
            ))
    for first, _ in steps:
        first.start()
    for first, second in steps:
        first.wait()
        second.start()
    for _, second in steps:
        second.wait()


def body(queries, keys, values, d_out, w_out, pattern, valid):
    tok, width = queries.shape[1], queries.shape[2]
    vm = pl.BlockSpec(memory_space=pltpu.VMEM)
    sm = pl.BlockSpec(memory_space=pltpu.SMEM)
    hbm = pl.BlockSpec(memory_space=pltpu.HBM)
    out = jax.ShapeDtypeStruct((1, tok, width), BF)
    dma = pltpu.SemaphoreType.DMA
    grads = pl.pallas_call(
        kernel,
        out_shape=(out, out, out),
        in_specs=[sm, sm, hbm, hbm, hbm, hbm, hbm],
        out_specs=(vm, vm, vm),
        scratch_shapes=[
            pltpu.VMEM((3, tok, width), BF),
            pltpu.VMEM((3, tok, width), BF),
            pltpu.VMEM((3, tok, width), BF),
            pltpu.VMEM((tok, D), BF),
            pltpu.VMEM((16, 4, 16, D), BF),
            pltpu.VMEM((2, HEADS, tok, HD), BF),
            pltpu.VMEM((2, HEADS, 8, 128), F32),
            pltpu.VMEM((HEADS, tok, HD), BF),
            pltpu.VMEM((HEADS, 8, 128), F32),
            pltpu.VMEM((HEADS, 3 * tok, tok), F32),
            pltpu.VMEM((HEADS, tok, HD), F32),
            pltpu.VMEM((HEADS, tok, HD), F32),
            pltpu.VMEM((3, tok, width), BF),
            dma((16, 4)),
            dma((2, 4, 3)),
            dma((6,)),
            dma((4, 4)),
            dma((2, 3)),
            dma((2, 3)),
            dma((2, HEADS)),
            dma((2, HEADS)),
            dma((2, HEADS)),
            dma((2, HEADS)),
            dma,
            dma((4,)),
            pltpu.SemaphoreType.REGULAR,
            dma((3,)),
        ],
        compiler_params=pltpu.CompilerParams(
            collective_id=0, has_side_effects=True
        ),
        name="attention_backward",
    )(pattern.T, valid, queries, keys, values, d_out, w_out.reshape(4, 16, D))
    hb = pl.BlockSpec(memory_space=pl.ANY)
    return pl.pallas_call(
        write_out,
        out_shape=(out, out, out),
        in_specs=[hb, hb, hb],
        out_specs=(hb, hb, hb),
        scratch_shapes=[pltpu.VMEM((3, tok, width), BF), dma((12,)), dma((12,))],
        name="write_out",
    )(*grads)


def solution(mesh):
    spec = P("fsdp", "seq", None)
    in_specs = (spec, spec, spec, spec, P("fsdp", None), P(), P("fsdp", None))
    return jax.shard_map(
        body, mesh=mesh, in_specs=in_specs, out_specs=(spec, spec, spec), check_vma=False
    )
```
